512 devices in a mesh: ctx: 64 (over x_lo, z, core), ch: 8 (over y, x_hi).
Axes of the slice: x: 4 (x_hi: 2, x_lo: 2; x = x_hi * 2 + x_lo), y: 4, z: 16, core: 2. Of those that a mesh axis runs over, the one named last changes fastest.
Arguments:
- streams: bfloat16 [3, 8192, 2048], P(None, 'ctx', 'ch'), may hold values from -6 to 6
- short_weight: float32 [3, 3, 2048], P(None, None, 'ch'), may hold values from -3 to 3
- filt_first: bfloat16 [2, 5, 64], replicated, may hold values from -2.5 to 2.5
- filt_bias: float32 [2, 2, 64], replicated, may hold values from -4 to 4
- filt_mid: bfloat16 [2, 64, 64], replicated, may hold values from -0.75 to 0.75
- filt_freq: float32 [2, 64], replicated, may hold values from 0.5 to 2
- filt_last: bfloat16 [2, 64, 2048], P(None, None, 'ch'), may hold values from -0.75 to 0.75
- decay: float32 [2, 2048], P(None, 'ch'), may hold values from 3.0517578e-05 to 0.03
- skip: float32 [2, 2048], P(None, 'ch'), may hold values from -4 to 4
- out_weight: bfloat16 [2048, 4096], P('ch'), may hold values from -0.125 to 0.125
Outputs:
- mixed: bfloat16 [8192, 4096], P('ctx', 'ch')
The draws below stay inside these ranges and needn't reach their ends.
All inputs are finite; a program needn't handle non-finite values.
Results may differ from the reference program's by a relative error of at most 0.01.
The reference program's roundings to bfloat16 on the way count: a program that leaves them out, or rounds other values in their place, can miss the bound.
Values may be sent and summed in bfloat16 or wider, within the bound.
A program may use at most 64 MiB of HBM per device.

```python
import math
import jax
import jax.numpy as jnp

D = 4096
CH = 2048
ORD = 64
EMB = 5
SEQ = 8192


def signed_draw(key, shape, limit):
    values = jax.random.uniform(jax.random.fold_in(key, 13), shape, jnp.float32, -limit, limit)
    return values


def draw_filt_first(key, part):
    values = signed_draw(jax.random.fold_in(key, 101), (2, EMB, ORD), 2.5)
    return values.astype(jnp.bfloat16)


def draw_filt_mid(key, part):
    values = signed_draw(jax.random.fold_in(key, 202), (2, ORD, ORD), 0.75)
    return values.astype(jnp.bfloat16)


def block_scale(key, shape, shards, low, high):
    loudness, own = 1.0, jax.random.fold_in(key, 6)
    for position, blocks in shards:
        heights = jnp.exp(jax.random.uniform(jax.random.fold_in(own, position), (blocks,), jnp.float32, low / len(shards), high / len(shards)))
        loudness = loudness * jnp.repeat(heights, shape[position] // blocks).reshape([-1 if axis == position else 1 for axis in range(len(shape))])
    return loudness


def gaussian(rng, dims, width, most, cuts=(), kind=jnp.bfloat16):
    drawn = width * jax.random.normal(rng, dims, jnp.float32)
    if cuts:
        drawn = drawn * block_scale(rng, dims, cuts, -0.22, 0.18)
    return jnp.clip(drawn, -most, most).astype(kind)


def setup_inputs(seed: int = 0) -> dict:
    splits = jax.random.split(jax.random.key(seed), 11)
    streams = gaussian(splits[0], (3, SEQ, CH), 1.0, 6.0, ((1, 64), (2, 8)))
    short_weight = gaussian(splits[1], (3, 3, CH), 0.6, 3.0, ((2, 8),), jnp.float32)
    filt_first = draw_filt_first(jax.random.fold_in(splits[10], 71), 0)
    filt_bias = gaussian(splits[3], (2, 2, ORD), 1.0, 4.0, (), jnp.float32)
    filt_mid = draw_filt_mid(jax.random.fold_in(splits[10], 71), 0)
    filt_freq = jnp.clip(jnp.exp(jax.random.uniform(splits[5], (2, ORD), jnp.float32, math.log(0.5), math.log(2.0))), 0.5, 2.0)
    filt_last = gaussian(splits[6], (2, ORD, CH), ORD ** -0.5, 0.75, ((2, 8),))
    decay = jnp.clip(jnp.exp(math.log(0.03) - 6.89065 * jax.random.uniform(splits[7], (2, CH), jnp.float32) ** block_scale(splits[7], (2, CH), ((1, 8),), -0.2, 0.2)), 3.0517578125e-05, 0.03)
    skip = gaussian(splits[8], (2, CH), 1.0, 4.0, ((1, 8),), jnp.float32)
    out_weight = gaussian(splits[9], (CH, D), CH ** -0.5, 0.125, ((0, 8),))
    return dict(streams=streams, short_weight=short_weight, filt_first=filt_first, filt_bias=filt_bias, filt_mid=filt_mid, filt_freq=filt_freq, filt_last=filt_last, decay=decay, skip=skip, out_weight=out_weight)


def features(positions, seq_len):
    bands = (EMB - 1) // 2
    cols = [positions.astype(jnp.float32) / seq_len]
    cosines = []
    sines = []
    for band in range(bands):
        wrapped = (band + 1) * positions % seq_len
        angle = 2.0 * math.pi / seq_len * wrapped.astype(jnp.float32)
        cosines.append(jnp.cos(angle))
        sines.append(jnp.sin(angle))
    return jnp.stack(cols + cosines + sines, axis=-1)

def filter_rows(positions, seq_len, first, bias, mid, freq, last, rate):
    feat = features(positions, seq_len).astype(jnp.bfloat16)
    act_one = jnp.sin(freq * (jnp.dot(feat, first, preferred_element_type=jnp.float32) + bias[0])).astype(jnp.bfloat16)
    act_two = jnp.sin(freq * (jnp.dot(act_one, mid, preferred_element_type=jnp.float32) + bias[1])).astype(jnp.bfloat16)
    raw = jnp.dot(act_two, last, preferred_element_type=jnp.float32)
    lagged = positions.astype(jnp.float32)[:, None]
    return raw * jnp.exp(-rate[None, :] * lagged) * jnp.sqrt(2.0 * rate)[None, :]

def reference(streams, short_weight, filt_first, filt_bias, filt_mid, filt_freq, filt_last, decay, skip, out_weight):
    values = streams.astype(jnp.float32)
    padded = jnp.pad(values, ((0, 0), (2, 0), (0, 0)))
    shortened = (short_weight[:, 0][:, None, :] * values + short_weight[:, 1][:, None, :] * padded[:, 1:-1] + short_weight[:, 2][:, None, :] * padded[:, :-2]).astype(jnp.bfloat16)
    positions = jnp.arange(SEQ, dtype=jnp.int32)
    state = shortened[0]
    for order in range(2):
        filt = filter_rows(positions, SEQ, filt_first[order], filt_bias[order], filt_mid[order], filt_freq[order], filt_last[order], decay[order])
        signal = state.astype(jnp.float32)
        spectrum = jnp.fft.rfft(filt, n=2 * SEQ, axis=0) * jnp.fft.rfft(signal, n=2 * SEQ, axis=0)
        conv = jnp.fft.irfft(spectrum, n=2 * SEQ, axis=0)[:SEQ]
        output = conv + skip[order][None, :] * signal
        state = (shortened[order + 1].astype(jnp.float32) * output).astype(jnp.bfloat16)
    return jnp.dot(state, out_weight, preferred_element_type=jnp.float32).astype(jnp.bfloat16)
```

```python
import functools
import math

import jax
import jax.numpy as jnp
import numpy as np
from jax import lax
from jax.experimental import pallas as pl
from jax.experimental.pallas import tpu as pltpu
from jax.sharding import PartitionSpec as P

MESH = pl.DeviceIdType.MESH
BF16 = jnp.bfloat16
F32 = jnp.float32
EMB = 5
LANES = 128


def split_table(table):
    high = table.astype(np.float32).astype(jnp.bfloat16)
    low = (table - high.astype(np.float64)).astype(np.float32).astype(jnp.bfloat16)
    return np.stack([high, low])


def transform_tables(rows, kept):
    total = 2 * rows * LANES
    k = np.arange(kept)[:, None]
    live = k <= rows
    a = np.arange(rows)[None, :]
    b = np.arange(LANES)[None, :]
    angle = 2.0 * np.pi * ((k * a) % (2 * rows)) / (2 * rows)
    cos_a = np.where(live, np.cos(angle), 0.0)
    sin_a = np.where(live, np.sin(angle), 0.0)
    first = np.concatenate([cos_a, -sin_a], axis=0)
    weight = np.where((k == 0) | (k == rows), 1.0, 2.0) / total
    last = np.concatenate([(weight * cos_a).T, (-weight * sin_a).T], axis=1)
    turn = 2.0 * np.pi * ((k * b) % total) / total
    twiddle = np.stack([np.cos(turn), -np.sin(turn)]).astype(np.float32)
    j = np.arange(LANES)[:, None]
    phase = 2.0 * np.pi * ((j * b) % LANES) / LANES
    cos_b, sin_b = np.cos(phase), np.sin(phase)
    forward = np.block([[cos_b, -sin_b], [sin_b, cos_b]])
    wide = np.concatenate([split_table(forward), split_table(forward.T)])
    return split_table(first), split_table(last), twiddle, wide


def feature_table(seq_len):
    positions = np.arange(seq_len, dtype=np.int32)
    rows = [positions.astype(np.float32) / np.float32(seq_len)]
    cosines, sines = [], []
    for band in range((EMB - 1) // 2):
        wrapped = (band + 1) * positions % seq_len
        angle = np.float32(2.0 * math.pi / seq_len) * wrapped.astype(np.float32)
        cosines.append(np.cos(angle))
        sines.append(np.sin(angle))
    table = np.zeros((8, seq_len), np.float32)
    table[:EMB] = np.stack(rows + cosines + sines)
    return table.astype(jnp.bfloat16)


def sine_terms():
    e = 0.25 * np.cos(np.pi * (np.arange(400) + 0.5) / 800)
    basis = np.stack([e ** (2 * i + 1) for i in range(5)], axis=1)
    scale = 1.0 / np.maximum(np.abs(np.sin(2 * np.pi * e)), 1e-3)
    terms = np.linalg.lstsq(basis * scale[:, None], np.sin(2 * np.pi * e) * scale, rcond=None)[0]
    return [float(np.float32(t)) for t in terms]


def dot(a, b):
    return jnp.dot(a, b, preferred_element_type=F32)


def dot_nt(a, b):
    return lax.dot_general(a, b, (((1,), (1,)), ((), ())), preferred_element_type=F32)


def halves(x):
    high = x.astype(BF16)
    return high, (x - high.astype(F32)).astype(BF16)


def eye(n, dtype):
    rows = lax.broadcasted_iota(jnp.int32, (n, n), 0)
    cols = lax.broadcasted_iota(jnp.int32, (n, n), 1)
    return (rows == cols).astype(F32).astype(dtype)


def column(row, n):
    rows = lax.broadcasted_iota(jnp.int32, (n, n), 0)
    cols = lax.broadcasted_iota(jnp.int32, (n, n), 1)
    return jnp.sum(jnp.where(rows == cols, row, 0.0), axis=1, keepdims=True)


def kernel(
    n_ctx,
    n_ch,
    chunk,
    sine,
    streams_in,
    short_in,
    first_in,
    bias_in,
    mid_in,
    freq_in,
    last_in,
    decay_in,
    skip_in,
    weight_in,
    lead_in,
    tail_in,
    twiddle_in,
    wide_in,
    feat_in,
    out_ref,
    streams,
    short,
    first,
    bias,
    mid,
    freq,
    last,
    decay,
    skip,
    lead,
    tail,
    twiddle,
    wide,
    feat,
    outgoing,
    incoming,
    stage,
    signal,
    filt,
    spectrum,
    back_out,
    back_in,
    gathered,
    weight,
    load_sem,
    send_sem,
    recv_sem,
    back_send,
    back_recv,
    ring_send,
    ring_recv,
    w_send,
    w_recv,
    pair_send,
    pair_recv,
):
    me = lax.axis_index("ctx")
    group = lax.axis_index("ch")
    half = lax.rem(me, 2)
    partner = me + 1 - 2 * half
    tok, chl = streams.shape[1], streams.shape[2]
    per = chl // n_ctx
    kept = twiddle.shape[1]
    seq_len = feat.shape[1]

    def ctx_peer(d):
        return lax.rem(me + d, n_ctx)

    def ch_peer(d):
        return lax.rem(group + d, n_ch)

    barrier = pltpu.get_barrier_semaphore()

    def greet_ctx(d, carry):
        pl.semaphore_signal(barrier, inc=1, device_id=(ctx_peer(d), group), device_id_type=MESH)
        return carry

    def greet_ch(d, carry):
        pl.semaphore_signal(barrier, inc=1, device_id=(me, ch_peer(d)), device_id_type=MESH)
        return carry

    lax.fori_loop(1, n_ctx, greet_ctx, 0)
    lax.fori_loop(1, n_ch, greet_ch, 0)

    loads = []
    pairs = (
        (streams_in, streams),
        (feat_in, feat),
        (first_in, first),
        (bias_in, bias),
        (mid_in, mid),
        (freq_in, freq),
        (last_in, last),
        (decay_in, decay),
        (lead_in, lead),
        (twiddle_in, twiddle),
        (wide_in, wide),
        (short_in, short),
        (skip_in, skip),
        (tail_in, tail),
    )
    for i, (src, dst) in enumerate(pairs):
        copy = pltpu.make_async_copy(src, dst, load_sem.at[i])
        copy.start()
        loads.append(copy)

    loads[0].wait()
    flip = eye(chl, BF16)
    for s in range(3):
        stage[...] = dot_nt(flip, streams[s])
        outgoing[s] = stage[...].reshape(n_ctx, per, tok).astype(BF16)

    for copy in loads[1:]:
        copy.wait()

    lane = lax.broadcasted_iota(jnp.int32, (1, chl), 1)

    def picked(row, c):
        return jnp.sum(jnp.where(lane == me * per + c, row, 0.0), axis=1, keepdims=True)

    pick_rows = lax.broadcasted_iota(jnp.int32, (8, chl), 0)
    pick_cols = lax.broadcasted_iota(jnp.int32, (8, chl), 1)
    pick = jnp.where((pick_rows < per) & (pick_cols == me * per + pick_rows), 1.0, 0.0)

    def make_filter(o):
        hidden = mid.shape[1]
        base = first[o].astype(F32)
        base = jnp.concatenate([base, jnp.zeros((8 - EMB, hidden), F32)], axis=0).astype(BF16)
        flip_h = eye(hidden, BF16)
        lift = dot_nt(flip_h, base).astype(BF16)
        mix = dot_nt(flip_h, mid[o]).astype(BF16)
        pull = dot_nt(pick.astype(BF16), last[o]).astype(BF16)
        rate_row = jnp.where(pick > 0.0, decay[o : o + 1, :], 0.0)
        rate = jnp.sum(rate_row, axis=1, keepdims=True)
        gain = jnp.sqrt(2.0 * rate)
        turns = column(freq[o : o + 1, :], hidden) * (1.0 / (2.0 * math.pi))
        shift_one = column(bias[o, 0:1, :], hidden) * turns - 0.25
        shift_two = column(bias[o, 1:2, :], hidden) * turns - 0.25

        def sine_of(pre, shift):
            t = pre * turns + shift
            e = 0.25 - jnp.abs(t - jnp.round(t))
            e2 = e * e
            acc = sine[-1]
            for term in sine[-2::-1]:
                acc = acc * e2 + term
            return (acc * e).astype(BF16)

        def step(i, carry):
            start = pl.multiple_of(i * chunk, chunk)
            act_one = sine_of(dot(lift, feat[:, pl.ds(start, chunk)]), shift_one)
            act_two = sine_of(dot(mix, act_one), shift_two)
            raw = dot(pull, act_two)
            lag = (lax.broadcasted_iota(jnp.int32, (8, chunk), 1) + start).astype(F32)
            value = raw * jnp.exp(-rate * lag) * gain
            for q in range(chunk // LANES):
                row = pl.multiple_of((i * (chunk // LANES) + q) * 8, 8)
                filt[pl.ds(row, 8), :] = value[:, q * LANES : (q + 1) * LANES]
            return carry

        lax.fori_loop(0, seq_len // chunk, step, 0)

    tw_re, tw_im = twiddle[0], twiddle[1]

    def forward(terms):
        high = terms[0]
        part = dot(lead[0], high) + dot(lead[1], high)
        if len(terms) > 1:
            part = part + dot(lead[0], terms[1])
        rows = []
        for c in range(per):
            re = part[:kept, c * LANES : (c + 1) * LANES]
            im = part[kept:, c * LANES : (c + 1) * LANES]
            rows.append(jnp.concatenate([re * tw_re - im * tw_im, re * tw_im + im * tw_re], axis=1))
        high, low = halves(jnp.concatenate(rows, axis=0))
        return dot(high, wide[0]) + dot(low, wide[0]) + dot(high, wide[1])

    def inverse(spec):
        high, low = halves(spec)
        part = dot(high, wide[2]) + dot(low, wide[2]) + dot(high, wide[3])
        cols = []
        for c in range(per):
            re = part[c * kept : (c + 1) * kept, :LANES]
            im = part[c * kept : (c + 1) * kept, LANES:]
            cols.append(jnp.concatenate([re * tw_re + im * tw_im, im * tw_re - re * tw_im], axis=0))
        high, low = halves(jnp.concatenate(cols, axis=1))
        return dot(tail[0], high) + dot(tail[0], low) + dot(tail[1], high)

    def make_spectrum(o):
        cols = [filt[pl.ds(c, n_ctx, stride=8), :] for c in range(per)]
        spectrum[o] = forward(halves(jnp.concatenate(cols, axis=1)))

    def convolve(o, state):
        spec = forward((state.astype(BF16),))
        re, im = spec[:, :LANES], spec[:, LANES:]
        f_re, f_im = spectrum[o, :, :LANES], spectrum[o, :, LANES:]
        return inverse(jnp.concatenate([re * f_re - im * f_im, re * f_im + im * f_re], axis=1))

    make_filter(0)
    make_spectrum(0)
    pl.semaphore_wait(barrier, n_ctx + n_ch - 2)

    for s in range(3):
        pltpu.make_async_copy(outgoing.at[s, me], incoming.at[s, me], recv_sem.at[s]).start()

        def send(d, carry):
            peer = ctx_peer(d)
            pltpu.make_async_remote_copy(
                src_ref=outgoing.at[s, peer],
                dst_ref=incoming.at[s, me],
                send_sem=send_sem.at[s],
                recv_sem=recv_sem.at[s],
                device_id=(peer, group),
                device_id_type=MESH,
            ).start()
            return carry

        lax.fori_loop(1, n_ctx, send, 0)

    depth, cols_out = weight.shape[2], weight.shape[3]

    def weight_block(g):
        return weight_in.at[
            pl.ds(pl.multiple_of(half * depth, depth), depth),
            pl.ds(pl.multiple_of(g * cols_out, cols_out), cols_out),
        ]

    pltpu.make_async_copy(weight_block(group), weight.at[group, half], w_recv).start()

    def send_weight(d, carry):
        peer = ch_peer(d)
        pltpu.make_async_remote_copy(
            src_ref=weight_block(peer),
            dst_ref=weight.at[group, half],
            send_sem=w_send,
            recv_sem=w_recv,
            device_id=(me, peer),
            device_id_type=MESH,
        ).start()
        return carry

    lax.fori_loop(1, n_ch, send_weight, 0)

    make_filter(1)
    make_spectrum(1)

    row0 = lax.broadcasted_iota(jnp.int32, (n_ctx, LANES), 0) == 0
    lane_at = lax.broadcasted_iota(jnp.int32, (n_ctx, LANES), 1)

    def delayed(x, by):
        near = pltpu.roll(x, by, 1)
        carried = jnp.where(row0, 0.0, pltpu.roll(near, 1, 0))
        return jnp.where(lane_at < by, carried, near)

    def shortened(s):
        pltpu.make_async_copy(incoming.at[s], incoming.at[s], recv_sem.at[s]).wait()
        signal[...] = incoming[s].astype(F32).reshape(n_ctx * per, tok)
        cols = []
        for c in range(per):
            x = signal[pl.ds(c, n_ctx, stride=per), :]
            taps = [picked(short[s, i : i + 1, :], c) for i in range(3)]
            cols.append(taps[0] * x + taps[1] * delayed(x, 1) + taps[2] * delayed(x, 2))
        return jnp.concatenate(cols, axis=1).astype(BF16).astype(F32)

    state = shortened(0)
    for o in range(2):
        direct = jnp.concatenate(
            [jnp.broadcast_to(picked(skip[o : o + 1, :], c), (1, LANES)) for c in range(per)], axis=1
        )
        output = convolve(o, state) + direct * state
        state = (shortened(o + 1) * output).astype(BF16).astype(F32)
    for c in range(per):
        stage[pl.ds(c, n_ctx, stride=per), :] = state[:, c * LANES : (c + 1) * LANES]
    back_out[...] = stage[...].reshape(n_ctx, per, tok).astype(BF16)

    pltpu.make_async_copy(back_out.at[me], back_in.at[me], back_recv).start()

    def send_back(d, carry):
        peer = ctx_peer(d)
        pltpu.make_async_remote_copy(
            src_ref=back_out.at[peer],
            dst_ref=back_in.at[me],
            send_sem=back_send,
            recv_sem=back_recv,
            device_id=(peer, group),
            device_id_type=MESH,
        ).start()
        return carry

    lax.fori_loop(1, n_ctx, send_back, 0)

    pltpu.make_async_copy(weight.at[:, half], weight.at[:, half], w_recv).wait()
    swap = pltpu.make_async_remote_copy(
        src_ref=weight.at[:, half],
        dst_ref=weight.at[:, half],
        send_sem=pair_send,
        recv_sem=pair_recv,
        device_id=(partner, group),
        device_id_type=MESH,
    )
    swap.start()

    pltpu.make_async_copy(back_in, back_in, back_recv).wait()
    signal[...] = back_in[...].astype(F32).reshape(n_ctx * per, tok)
    mine = dot_nt(eye(tok, BF16), signal[...].astype(BF16)).astype(BF16)
    gathered[group] = mine

    def send_ring(d, carry):
        pltpu.make_async_remote_copy(
            src_ref=gathered.at[group],
            dst_ref=gathered.at[group],
            send_sem=ring_send,
            recv_sem=ring_recv.at[group],
            device_id=(me, ch_peer(d)),
            device_id_type=MESH,
        ).start()
        return carry

    lax.fori_loop(1, n_ch, send_ring, 0)
    swap.wait()

    def product(g, rows):
        return dot(rows, weight[g].reshape(2 * depth, cols_out))

    total = product(group, mine)
    for d in range(1, n_ch):
        peer = ch_peer(d)
        pltpu.make_async_copy(gathered.at[peer], gathered.at[peer], ring_recv.at[peer]).wait()
        total = total + product(peer, gathered[peer])
    out_ref[...] = total.astype(BF16)

    for s in range(3):
        sent = outgoing.at[s, pl.ds(0, n_ctx - 1)]
        pltpu.make_async_copy(sent, sent, send_sem.at[s]).wait()
    sent = back_out.at[pl.ds(0, n_ctx - 1)]
    pltpu.make_async_copy(sent, sent, back_send).wait()
    sent = gathered.at[pl.ds(0, n_ch - 1)]
    pltpu.make_async_copy(sent, sent, ring_send).wait()
    sent = weight.at[pl.ds(0, n_ch - 1), half]
    pltpu.make_async_copy(sent, sent, w_send).wait()


def solution(mesh):
    n_ctx, n_ch = mesh.shape["ctx"], mesh.shape["ch"]

    def per_device(
        streams,
        short_weight,
        filt_first,
        filt_bias,
        filt_mid,
        filt_freq,
        filt_last,
        decay,
        skip,
        out_weight,
    ):
        tok, chl = streams.shape[1], streams.shape[2]
        per = chl // n_ctx
        seq_len = tok * n_ctx
        kept = (n_ctx + 1 + 7) // 8 * 8
        cols_out = out_weight.shape[1] // n_ch
        lead, tail, twiddle, wide = transform_tables(n_ctx, kept)
        feat = feature_table(seq_len)
        args = (
            streams,
            short_weight,
            filt_first,
            filt_bias,
            filt_mid,
            filt_freq,
            filt_last,
            decay,
            skip,
            out_weight,
            jnp.asarray(lead),
            jnp.asarray(tail),
            jnp.asarray(twiddle),
            jnp.asarray(wide),
            jnp.asarray(feat),
        )

        def vmem(x):
            return pltpu.VMEM(x.shape, x.dtype)

        staged = [vmem(args[i]) for i in (0, 1, 2, 3, 4, 5, 6, 7, 8, 10, 11, 12, 13, 14)]
        dma = pltpu.SemaphoreType.DMA
        return pl.pallas_call(
            functools.partial(kernel, n_ctx, n_ch, min(1024, seq_len), sine_terms()),
            out_shape=jax.ShapeDtypeStruct((tok, cols_out), BF16),
            in_specs=[pl.BlockSpec(memory_space=pl.ANY)] * len(args),
            out_specs=pl.BlockSpec(memory_space=pltpu.VMEM),
            scratch_shapes=staged
            + [
                pltpu.VMEM((3, n_ctx, per, tok), BF16),
                pltpu.VMEM((3, n_ctx, per, tok), BF16),
                pltpu.VMEM((chl, tok), F32),
                pltpu.VMEM((chl, tok), F32),
                pltpu.VMEM((n_ctx * 8, LANES), F32),
                pltpu.VMEM((2, per * kept, 2 * LANES), F32),
                pltpu.VMEM((n_ctx, per, tok), BF16),
                pltpu.VMEM((n_ctx, per, tok), BF16),
                pltpu.VMEM((n_ch, tok, chl), BF16),
                pltpu.VMEM((n_ch, 2, chl // 2, cols_out), BF16),
                dma((14,)),
                dma((3,)),
                dma((3,)),
                dma,
                dma,
                dma,
                dma((n_ch,)),
                dma,
                dma,
                dma,
                dma,
            ],
            compiler_params=pltpu.CompilerParams(collective_id=0, has_side_effects=True),
        )(*args)

    return jax.shard_map(
        per_device,
        mesh=mesh,
        in_specs=(
            P(None, "ctx", "ch"),
            P(None, None, "ch"),
            P(),
            P(),
            P(),
            P(),
            P(None, None, "ch"),
            P(None, "ch"),
            P(None, "ch"),
            P("ch", None),
        ),
        out_specs=P("ctx", "ch"),
        check_vma=False,
    )
```

```python
import functools
import math

import jax
import jax.numpy as jnp
import numpy as np
from jax import lax
from jax.experimental import pallas as pl
from jax.experimental.pallas import tpu as pltpu
from jax.sharding import PartitionSpec as P

MESH = pl.DeviceIdType.MESH
BF16 = jnp.bfloat16
F32 = jnp.float32
EMB = 5
LANES = 128


def split_table(table):
    high = table.astype(np.float32).astype(jnp.bfloat16)
    low = (table - high.astype(np.float64)).astype(np.float32).astype(jnp.bfloat16)
    return np.stack([high, low])


def transform_tables(rows, kept):
    total = 2 * rows * LANES
    k = np.arange(kept)[:, None]
    live = k <= rows
    a = np.arange(rows)[None, :]
    b = np.arange(LANES)[None, :]
    angle = 2.0 * np.pi * ((k * a) % (2 * rows)) / (2 * rows)
    cos_a = np.where(live, np.cos(angle), 0.0)
    sin_a = np.where(live, np.sin(angle), 0.0)
    first = np.concatenate([cos_a, -sin_a], axis=0)
    weight = np.where((k == 0) | (k == rows), 1.0, 2.0) / total
    last = np.concatenate([(weight * cos_a).T, (-weight * sin_a).T], axis=1)
    turn = 2.0 * np.pi * ((k * b) % total) / total
    twiddle = np.stack([np.cos(turn), -np.sin(turn)]).astype(np.float32)
    j = np.arange(LANES)[:, None]
    phase = 2.0 * np.pi * ((j * b) % LANES) / LANES
    cos_b, sin_b = np.cos(phase), np.sin(phase)
    forward = np.block([[cos_b, -sin_b], [sin_b, cos_b]])
    wide = np.concatenate([split_table(forward), split_table(forward.T)])
    return split_table(first), split_table(last), twiddle, wide


def feature_table(seq_len):
    positions = np.arange(seq_len, dtype=np.int32)
    rows = [positions.astype(np.float32) / np.float32(seq_len)]
    cosines, sines = [], []
    for band in range((EMB - 1) // 2):
        wrapped = (band + 1) * positions % seq_len
        angle = np.float32(2.0 * math.pi / seq_len) * wrapped.astype(np.float32)
        cosines.append(np.cos(angle))
        sines.append(np.sin(angle))
    table = np.zeros((8, seq_len), np.float32)
    table[:EMB] = np.stack(rows + cosines + sines)
    table[EMB] = 1.0
    return np.concatenate([table] * 3).astype(jnp.bfloat16)


def sine_terms():
    e = 0.25 * np.cos(np.pi * (np.arange(400) + 0.5) / 800)
    basis = np.stack([e ** (2 * i + 1) for i in range(4)], axis=1)
    scale = 1.0 / np.maximum(np.abs(np.sin(2 * np.pi * e)), 1e-3)
    terms = np.linalg.lstsq(basis * scale[:, None], np.sin(2 * np.pi * e) * scale, rcond=None)[0]
    return [float(np.float32(t)) for t in terms]


def dot(a, b):
    return jnp.dot(a, b, preferred_element_type=F32)


def dot_nt(a, b):
    return lax.dot_general(a, b, (((1,), (1,)), ((), ())), preferred_element_type=F32)


def halves(x):
    high = x.astype(BF16)
    return high, (x - high.astype(F32)).astype(BF16)


def eye(n, dtype):
    rows = lax.broadcasted_iota(jnp.int32, (n, n), 0)
    cols = lax.broadcasted_iota(jnp.int32, (n, n), 1)
    return (rows == cols).astype(F32).astype(dtype)


def terms(x, count):
    parts = []
    for _ in range(count):
        part = x.astype(BF16).astype(F32)
        parts.append(part)
        x = x - part
    return parts


def kernel(
    n_ctx,
    n_ch,
    chunk,
    sine,
    streams_in,
    short_in,
    first_in,
    bias_in,
    mid_in,
    freq_in,
    last_in,
    decay_in,
    skip_in,
    weight_in,
    lead_in,
    tail_in,
    twiddle_in,
    wide_in,
    feat_in,
    out_ref,
    streams,
    short,
    first,
    bias,
    mid,
    freq,
    last,
    decay,
    skip,
    lead,
    tail,
    twiddle,
    wide,
    feat,
    outgoing,
    incoming,
    signal,
    filt,
    spectrum,
    back_out,
    back_in,
    gathered,
    weight,
    load_sem,
    send_sem,
    recv_sem,
    back_send,
    back_recv,
    ring_send,
    ring_recv,
    w_send,
    w_recv,
    pair_send,
    pair_recv,
    filt_send,
    filt_recv,
):
    me = lax.axis_index("ctx")
    group = lax.axis_index("ch")
    half = lax.rem(me, 2)
    partner = me + 1 - 2 * half
    tok, chl = streams.shape[1], streams.shape[2]
    wide_half = chl // 2
    kept = twiddle.shape[1]
    seq_len = feat.shape[1]

    def ctx_peer(d):
        return lax.rem(me + d, n_ctx)

    def ch_peer(d):
        return lax.rem(group + d, n_ch)

    def for_ctx_peers(act):
        quarter = n_ctx // 4
        act(ctx_peer(quarter))
        act(ctx_peer(3 * quarter))

        def step(e, carry):
            act(ctx_peer(quarter + e))
            act(ctx_peer(quarter - e))
            act(ctx_peer(3 * quarter + e))
            act(ctx_peer(3 * quarter - e))
            return carry

        lax.fori_loop(1, quarter, step, 0)
        act(ctx_peer(2 * quarter))

    loads = []
    pairs = (
        (streams_in, streams),
        (feat_in, feat),
        (first_in, first),
        (bias_in, bias),
        (mid_in, mid),
        (freq_in, freq),
        (last_in, last),
        (decay_in, decay),
        (lead_in, lead),
        (twiddle_in, twiddle),
        (wide_in, wide),
        (short_in, short),
        (skip_in, skip),
        (tail_in, tail),
    )
    for i, (src, dst) in enumerate(pairs):
        copy = pltpu.make_async_copy(src, dst, load_sem.at[i])
        copy.start()
        loads.append(copy)

    barrier = pltpu.get_barrier_semaphore()

    def greet_ctx(peer):
        pl.semaphore_signal(barrier, inc=1, device_id=(peer, group), device_id_type=MESH)

    for_ctx_peers(greet_ctx)
    for d in range(1, n_ch):
        pl.semaphore_signal(barrier, inc=1, device_id=(me, ch_peer(d)), device_id_type=MESH)

    loads[0].wait()
    flip = eye(tok, BF16)
    for h in range(2):
        for s in range(3):
            block = streams[s, :, h * wide_half : (h + 1) * wide_half]
            turned = dot_nt(eye(wide_half, BF16), block)
            outgoing[h, :, s] = turned.reshape(n_ctx, 2, tok).astype(BF16)

    pl.semaphore_wait(barrier, n_ctx + n_ch - 2)

    for h in range(2):
        pltpu.make_async_copy(outgoing.at[h, me], incoming.at[h, me], recv_sem.at[h]).start()

        def send(peer):
            pltpu.make_async_remote_copy(
                src_ref=outgoing.at[h, peer],
                dst_ref=incoming.at[h, me],
                send_sem=send_sem.at[h],
                recv_sem=recv_sem.at[h],
                device_id=(peer, group),
                device_id_type=MESH,
            ).start()

        for_ctx_peers(send)

    depth, cols_out = weight.shape[2], weight.shape[3]

    def weight_block(g):
        return weight_in.at[
            pl.ds(pl.multiple_of(half * depth, depth), depth),
            pl.ds(pl.multiple_of(g * cols_out, cols_out), cols_out),
        ]

    pltpu.make_async_copy(weight_block(group), weight.at[group, half], w_recv).start()
    for d in range(1, n_ch):
        pltpu.make_async_remote_copy(
            src_ref=weight_block(ch_peer(d)),
            dst_ref=weight.at[group, half],
            send_sem=w_send,
            recv_sem=w_recv,
            device_id=(me, ch_peer(d)),
            device_id_type=MESH,
        ).start()

    for copy in loads[1:]:
        copy.wait()

    lane = lax.broadcasted_iota(jnp.int32, (1, chl), 1)

    def place(owner, c):
        return (c // 2) * wide_half + 2 * owner + c % 2

    def picked(row, c):
        return jnp.sum(jnp.where(lane == place(me, c), row, 0.0), axis=1, keepdims=True)

    pick_rows = lax.broadcasted_iota(jnp.int32, (8, chl), 0)
    pick_cols = lax.broadcasted_iota(jnp.int32, (8, chl), 1)
    pick = jnp.zeros((8, chl), F32)
    for r in range(8):
        here = (pick_rows == r) & (pick_cols == place(me - half + r // 4, r % 4))
        pick = jnp.where(here, 1.0, pick)

    hidden = mid.shape[1]
    turns = freq[pl.ds(half, 1), :] * (1.0 / (2.0 * math.pi))
    both = first[...].astype(F32)
    base = jnp.where(half == 0, both[:, 0, :], both[:, 1, :]) * turns
    shifts = bias[half] * turns - 0.25
    base = jnp.concatenate([base, shifts[0:1], jnp.zeros((8 - EMB - 1, hidden), F32)], axis=0)
    flip_h = eye(hidden, BF16)
    lift = dot_nt(flip_h, jnp.concatenate(terms(base, 3), axis=0).astype(BF16)).astype(BF16)
    mixed = terms(mid[half].astype(F32) * turns, 2)
    mixed = mixed + terms(shifts[1:2], 3) + [jnp.zeros((13, hidden), F32)]
    mix = dot_nt(flip_h, jnp.concatenate(mixed, axis=0).astype(BF16)).astype(BF16)
    pull = dot_nt(pick.astype(BF16), last[half]).astype(BF16)
    rate_row = jnp.where(pick > 0.0, decay[pl.ds(half, 1), :], 0.0)
    rate = jnp.sum(rate_row, axis=1, keepdims=True)
    gain = jnp.sqrt(2.0 * rate)
    ones = (lax.broadcasted_iota(jnp.int32, (16, chunk), 0) < 3).astype(F32).astype(BF16)

    def sine_of(t):
        e = 0.25 - jnp.abs(t - jnp.round(t))
        e2 = e * e
        acc = sine[-1]
        for term in sine[-2::-1]:
            acc = acc * e2 + term
        return (acc * e).astype(BF16)

    def filter_step(i, carry):
        start = pl.multiple_of(i * chunk, chunk)
        act_one = sine_of(dot(lift, feat[:, pl.ds(start, chunk)]))
        act_two = sine_of(dot(mix, jnp.concatenate([act_one, act_one, ones], axis=0)))
        raw = dot(pull, act_two)
        lag = (lax.broadcasted_iota(jnp.int32, (8, chunk), 1) + start).astype(F32)
        value = raw * jnp.exp(-rate * lag) * gain
        for q in range(chunk // LANES):
            row = pl.multiple_of((i * (chunk // LANES) + q) * 8, 8)
            filt[half, pl.ds(row, 8), :] = value[:, q * LANES : (q + 1) * LANES]
        part = filt.at[half, pl.ds(pl.multiple_of(i * (chunk // 16), chunk // 16), chunk // 16)]
        pltpu.make_async_remote_copy(
            src_ref=part,
            dst_ref=part,
            send_sem=filt_send,
            recv_sem=filt_recv,
            device_id=(partner, group),
            device_id_type=MESH,
        ).start()
        return carry

    lax.fori_loop(0, seq_len // chunk, filter_step, 0)

    tw_re, tw_im = twiddle[0], twiddle[1]

    def forward(parts):
        high = parts[0]
        part = dot(lead[0], high) + dot(lead[1], high)
        if len(parts) > 1:
            part = part + dot(lead[0], parts[1])
        rows = []
        for c in range(high.shape[1] // LANES):
            re = part[:kept, c * LANES : (c + 1) * LANES]
            im = part[kept:, c * LANES : (c + 1) * LANES]
            rows.append(jnp.concatenate([re * tw_re - im * tw_im, re * tw_im + im * tw_re], axis=1))
        high, low = halves(jnp.concatenate(rows, axis=0))
        return dot(high, wide[0]) + dot(low, wide[0]) + dot(high, wide[1])

    def inverse(spec):
        high, low = halves(spec)
        part = dot(high, wide[2]) + dot(low, wide[2]) + dot(high, wide[3])
        cols = []
        for c in range(spec.shape[0] // kept):
            re = part[c * kept : (c + 1) * kept, :LANES]
            im = part[c * kept : (c + 1) * kept, LANES:]
            cols.append(jnp.concatenate([re * tw_re + im * tw_im, im * tw_re - re * tw_im], axis=0))
        high, low = halves(jnp.concatenate(cols, axis=1))
        return dot(tail[0], high) + dot(tail[0], low) + dot(tail[1], high)

    def make_spectrum(o):
        cols = [filt[o, pl.ds(4 * half + c, n_ctx, stride=8), :] for c in range(4)]
        spectrum[o] = forward(halves(jnp.concatenate(cols, axis=1)))

    make_spectrum(half)
    sent = filt.at[half]
    pltpu.make_async_copy(sent, sent, filt_send).wait()
    came = filt.at[1 - half]
    pltpu.make_async_copy(came, came, filt_recv).wait()
    make_spectrum(1 - half)

    def convolve(o, h, state):
        spec = forward((state.astype(BF16),))
        re, im = spec[:, :LANES], spec[:, LANES:]
        rows = slice(2 * h * kept, 2 * (h + 1) * kept)
        f_re, f_im = spectrum[o, rows, :LANES], spectrum[o, rows, LANES:]
        return inverse(jnp.concatenate([re * f_re - im * f_im, re * f_im + im * f_re], axis=1))

    row0 = lax.broadcasted_iota(jnp.int32, (n_ctx, LANES), 0) == 0
    lane_at = lax.broadcasted_iota(jnp.int32, (n_ctx, LANES), 1)

    def delayed(x, by):
        near = pltpu.roll(x, by, 1)
        carried = jnp.where(row0, 0.0, pltpu.roll(near, 1, 0))
        return jnp.where(lane_at < by, carried, near)

    def shortened(h, s):
        signal[h, s] = incoming[h, :, s].astype(F32).reshape(n_ctx * 2, tok)
        cols = []
        for c in range(2):
            x = signal[h, s, pl.ds(c, n_ctx, stride=2), :]
            taps = [picked(short[s, i : i + 1, :], 2 * h + c) for i in range(3)]
            cols.append(taps[0] * x + taps[1] * delayed(x, 1) + taps[2] * delayed(x, 2))
        return jnp.concatenate(cols, axis=1).astype(BF16).astype(F32)

    for h in range(2):
        pltpu.make_async_copy(incoming.at[h], incoming.at[h], recv_sem.at[h]).wait()
        state = shortened(h, 0)
        for o in range(2):
            direct = jnp.concatenate(
                [jnp.broadcast_to(picked(skip[o : o + 1, :], 2 * h + c), (1, LANES)) for c in range(2)],
                axis=1,
            )
            output = convolve(o, h, state) + direct * state
            state = (shortened(h, o + 1) * output).astype(BF16).astype(F32)
        for c in range(2):
            signal[h, 0, pl.ds(c, n_ctx, stride=2), :] = state[:, c * LANES : (c + 1) * LANES]
        back_out[h] = signal[h, 0].reshape(n_ctx, 2, tok).astype(BF16)

        pltpu.make_async_copy(back_out.at[h, me], back_in.at[h, me], back_recv.at[h]).start()

        def send_back(peer):
            pltpu.make_async_remote_copy(
                src_ref=back_out.at[h, peer],
                dst_ref=back_in.at[h, me],
                send_sem=back_send.at[h],
                recv_sem=back_recv.at[h],
                device_id=(peer, group),
                device_id_type=MESH,
            ).start()

        for_ctx_peers(send_back)

    pltpu.make_async_copy(weight.at[:, half], weight.at[:, half], w_recv).wait()
    swap = pltpu.make_async_remote_copy(
        src_ref=weight.at[:, half],
        dst_ref=weight.at[:, half],
        send_sem=pair_send,
        recv_sem=pair_recv,
        device_id=(partner, group),
        device_id_type=MESH,
    )
    swap.start()

    for h in range(2):
        pltpu.make_async_copy(back_in.at[h], back_in.at[h], back_recv.at[h]).wait()
        block = back_in[h].astype(F32).reshape(n_ctx * 2, tok)
        gathered[h, group] = dot_nt(flip, block.astype(BF16)).astype(BF16)
        for d in range(1, n_ch):
            pltpu.make_async_remote_copy(
                src_ref=gathered.at[h, group],
                dst_ref=gathered.at[h, group],
                send_sem=ring_send.at[h],
                recv_sem=ring_recv.at[h, group],
                device_id=(me, ch_peer(d)),
                device_id_type=MESH,
            ).start()

    swap.wait()

    total = jnp.zeros((tok, cols_out), F32)
    for h in range(2):
        for d in range(n_ch):
            peer = ch_peer(d)
            if d > 0:
                came = gathered.at[h, peer]
                pltpu.make_async_copy(came, came, ring_recv.at[h, peer]).wait()
            total = total + dot(gathered[h, peer], weight[peer, h])
    out_ref[...] = total.astype(BF16)

    for h in range(2):
        sent = outgoing.at[h, pl.ds(0, n_ctx - 1)]
        pltpu.make_async_copy(sent, sent, send_sem.at[h]).wait()
        sent = back_out.at[h, pl.ds(0, n_ctx - 1)]
        pltpu.make_async_copy(sent, sent, back_send.at[h]).wait()
        sent = gathered.at[h, pl.ds(0, n_ch - 1)]
        pltpu.make_async_copy(sent, sent, ring_send.at[h]).wait()
    sent = weight.at[pl.ds(0, n_ch - 1), half]
    pltpu.make_async_copy(sent, sent, w_send).wait()


def solution(mesh):
    n_ctx, n_ch = mesh.shape["ctx"], mesh.shape["ch"]

    def per_device(
        streams,
        short_weight,
        filt_first,
        filt_bias,
        filt_mid,
        filt_freq,
        filt_last,
        decay,
        skip,
        out_weight,
    ):
        tok, chl = streams.shape[1], streams.shape[2]
        seq_len = tok * n_ctx
        kept = (n_ctx + 1 + 7) // 8 * 8
        cols_out = out_weight.shape[1] // n_ch
        lead, tail, twiddle, wide = transform_tables(n_ctx, kept)
        feat = feature_table(seq_len)
        args = (
            streams,
            short_weight,
            jnp.transpose(filt_first, (1, 0, 2)),
            filt_bias,
            filt_mid,
            filt_freq,
            filt_last,
            decay,
            skip,
            out_weight,
            jnp.asarray(lead),
            jnp.asarray(tail),
            jnp.asarray(twiddle),
            jnp.asarray(wide),
            jnp.asarray(feat),
        )

        def vmem(x):
            return pltpu.VMEM(x.shape, x.dtype)

        staged = [vmem(args[i]) for i in (0, 1, 2, 3, 4, 5, 6, 7, 8, 10, 11, 12, 13, 14)]
        dma = pltpu.SemaphoreType.DMA
        return pl.pallas_call(
            functools.partial(kernel, n_ctx, n_ch, min(512, seq_len), sine_terms()),
            out_shape=jax.ShapeDtypeStruct((tok, cols_out), BF16),
            in_specs=[pl.BlockSpec(memory_space=pl.ANY)] * len(args),
            out_specs=pl.BlockSpec(memory_space=pltpu.VMEM),
            scratch_shapes=staged
            + [
                pltpu.VMEM((2, n_ctx, 3, 2, tok), BF16),
                pltpu.VMEM((2, n_ctx, 3, 2, tok), BF16),
                pltpu.VMEM((2, 3, n_ctx * 2, tok), F32),
                pltpu.VMEM((2, n_ctx * 8, LANES), F32),
                pltpu.VMEM((2, 4 * kept, 2 * LANES), F32),
                pltpu.VMEM((2, n_ctx, 2, tok), BF16),
                pltpu.VMEM((2, n_ctx, 2, tok), BF16),
                pltpu.VMEM((2, n_ch, tok, chl // 2), BF16),
                pltpu.VMEM((n_ch, 2, chl // 2, cols_out), BF16),
                dma((14,)),
                dma((2,)),
                dma((2,)),
                dma((2,)),
                dma((2,)),
                dma((2,)),
                dma((2, n_ch)),
                dma,
                dma,
                dma,
                dma,
                dma,
                dma,
            ],
            compiler_params=pltpu.CompilerParams(collective_id=0, has_side_effects=True),
        )(*args)

    return jax.shard_map(
        per_device,
        mesh=mesh,
        in_specs=(
            P(None, "ctx", "ch"),
            P(None, None, "ch"),
            P(),
            P(),
            P(),
            P(),
            P(None, None, "ch"),
            P(None, "ch"),
            P(None, "ch"),
            P("ch", None),
        ),
        out_specs=P("ctx", "ch"),
        check_vma=False,
    )
```

```python
import functools
import math

import jax
import jax.numpy as jnp
import numpy as np
from jax import lax
from jax.experimental import pallas as pl
from jax.experimental.pallas import tpu as pltpu
from jax.sharding import PartitionSpec as P

MESH = pl.DeviceIdType.MESH
BF16 = jnp.bfloat16
F32 = jnp.float32
EMB = 5
LANES = 128


def split_table(table):
    high = table.astype(np.float32).astype(jnp.bfloat16)
    low = (table - high.astype(np.float64)).astype(np.float32).astype(jnp.bfloat16)
    return np.stack([high, low])


def transform_tables(rows, kept):
    total = 2 * rows * LANES
    k = np.arange(kept)[:, None]
    live = k <= rows
    a = np.arange(rows)[None, :]
    b = np.arange(LANES)[None, :]
    angle = 2.0 * np.pi * ((k * a) % (2 * rows)) / (2 * rows)
    cos_a = np.where(live, np.cos(angle), 0.0)
    sin_a = np.where(live, np.sin(angle), 0.0)
    first = np.concatenate([cos_a, -sin_a], axis=0)
    weight = np.where((k == 0) | (k == rows), 1.0, 2.0) / total
    last = np.concatenate([(weight * cos_a).T, (-weight * sin_a).T], axis=1)
    turn = 2.0 * np.pi * ((k * b) % total) / total
    twiddle = np.stack([np.cos(turn), -np.sin(turn)]).astype(np.float32)
    j = np.arange(LANES)[:, None]
    phase = 2.0 * np.pi * ((j * b) % LANES) / LANES
    cos_b, sin_b = np.cos(phase), np.sin(phase)
    forward = np.block([[cos_b, -sin_b], [sin_b, cos_b]])
    wide = np.concatenate([split_table(forward), split_table(forward.T)])
    return split_table(first), split_table(last), twiddle, wide


def feature_table(seq_len):
    positions = np.arange(seq_len, dtype=np.int32)
    rows = [positions.astype(np.float32) / np.float32(seq_len)]
    cosines, sines = [], []
    for band in range((EMB - 1) // 2):
        wrapped = (band + 1) * positions % seq_len
        angle = np.float32(2.0 * math.pi / seq_len) * wrapped.astype(np.float32)
        cosines.append(np.cos(angle))
        sines.append(np.sin(angle))
    table = np.zeros((8, seq_len), np.float32)
    table[:EMB] = np.stack(rows + cosines + sines)
    table[EMB] = 1.0
    return np.concatenate([table] * 3).astype(jnp.bfloat16)


def sine_terms():
    e = 0.25 * np.cos(np.pi * (np.arange(400) + 0.5) / 800)
    basis = np.stack([e ** (2 * i + 1) for i in range(4)], axis=1)
    scale = 1.0 / np.maximum(np.abs(np.sin(2 * np.pi * e)), 1e-3)
    terms = np.linalg.lstsq(basis * scale[:, None], np.sin(2 * np.pi * e) * scale, rcond=None)[0]
    return [float(np.float32(t)) for t in terms]


def dot(a, b):
    return jnp.dot(a, b, preferred_element_type=F32)


def dot_nt(a, b):
    return lax.dot_general(a, b, (((1,), (1,)), ((), ())), preferred_element_type=F32)


def halves(x):
    high = x.astype(BF16)
    return high, (x - high.astype(F32)).astype(BF16)


def eye(n, dtype):
    rows = lax.broadcasted_iota(jnp.int32, (n, n), 0)
    cols = lax.broadcasted_iota(jnp.int32, (n, n), 1)
    return (rows == cols).astype(F32).astype(dtype)


def terms(x, count):
    parts = []
    for _ in range(count):
        part = x.astype(BF16).astype(F32)
        parts.append(part)
        x = x - part
    return parts


def kernel(
    n_ctx,
    n_ch,
    chunk,
    sine,
    streams_in,
    short_in,
    first_in,
    bias_in,
    mid_in,
    freq_in,
    last_in,
    decay_in,
    skip_in,
    weight_in,
    lead_in,
    tail_in,
    twiddle_in,
    wide_in,
    feat_in,
    out_ref,
    streams,
    short,
    first,
    bias,
    mid,
    freq,
    last,
    decay,
    skip,
    lead,
    tail,
    twiddle,
    wide,
    feat,
    outgoing,
    incoming,
    signal,
    filt,
    spectrum,
    back_out,
    back_in,
    gathered,
    weight,
    halo,
    gate,
    load_sem,
    send_sem,
    recv_sem,
    back_send,
    back_recv,
    ring_send,
    ring_recv,
    w_send,
    w_recv,
    pair_send,
    pair_recv,
    filt_send,
    filt_recv,
    halo_send,
    halo_recv,
):
    me = lax.axis_index("ctx")
    group = lax.axis_index("ch")
    half = lax.rem(me, 2)
    partner = me + 1 - 2 * half
    tok, chl = streams.shape[1], streams.shape[2]
    wide_half = chl // 2
    kept = twiddle.shape[1]
    seq_len = feat.shape[1]

    def ctx_peer(d):
        return lax.rem(me + d, n_ctx)

    def ch_peer(d):
        return lax.rem(group + d, n_ch)

    def for_ctx_peers(act):
        quarter = n_ctx // 4
        act(ctx_peer(quarter))
        act(ctx_peer(3 * quarter))

        def step(e, carry):
            act(ctx_peer(quarter + e))
            act(ctx_peer(quarter - e))
            act(ctx_peer(3 * quarter + e))
            act(ctx_peer(3 * quarter - e))
            return carry

        lax.fori_loop(1, quarter, step, 0)
        act(ctx_peer(2 * quarter))

    loads = []
    pairs = (
        (streams_in, streams),
        (feat_in, feat),
        (first_in, first),
        (bias_in, bias),
        (mid_in, mid),
        (freq_in, freq),
        (last_in, last),
        (decay_in, decay),
        (lead_in, lead),
        (twiddle_in, twiddle),
        (wide_in, wide),
        (short_in, short),
        (skip_in, skip),
        (tail_in, tail),
    )
    for i, (src, dst) in enumerate(pairs):
        copy = pltpu.make_async_copy(src, dst, load_sem.at[i])
        copy.start()
        loads.append(copy)

    barrier = pltpu.get_barrier_semaphore()

    def greet_ctx(peer):
        pl.semaphore_signal(barrier, inc=1, device_id=(peer, group), device_id_type=MESH)

    for_ctx_peers(greet_ctx)
    for d in range(1, n_ch):
        pl.semaphore_signal(barrier, inc=1, device_id=(me, ch_peer(d)), device_id_type=MESH)

    loads[0].wait()
    flip = eye(tok, BF16)
    for h in range(2):
        for s in range(2):
            block = streams[s, :, h * wide_half : (h + 1) * wide_half]
            turned = dot_nt(eye(wide_half, BF16), block)
            outgoing[h, :, s] = turned.reshape(n_ctx, 2, tok).astype(BF16)

    pl.semaphore_wait(barrier, n_ctx + n_ch - 2)

    for h in range(2):
        pltpu.make_async_copy(outgoing.at[h, me], incoming.at[h, me], recv_sem.at[h]).start()

        def send(peer):
            pltpu.make_async_remote_copy(
                src_ref=outgoing.at[h, peer],
                dst_ref=incoming.at[h, me],
                send_sem=send_sem.at[h],
                recv_sem=recv_sem.at[h],
                device_id=(peer, group),
                device_id_type=MESH,
            ).start()

        for_ctx_peers(send)

    pltpu.make_async_remote_copy(
        src_ref=streams.at[2, pl.ds(tok - 8, 8)],
        dst_ref=halo,
        send_sem=halo_send,
        recv_sem=halo_recv,
        device_id=(ctx_peer(1), group),
        device_id_type=MESH,
    ).start()

    depth, cols_out = weight.shape[2], weight.shape[3]

    def weight_block(g):
        return weight_in.at[
            pl.ds(pl.multiple_of(half * depth, depth), depth),
            pl.ds(pl.multiple_of(g * cols_out, cols_out), cols_out),
        ]

    pltpu.make_async_copy(weight_block(group), weight.at[group, half], w_recv).start()
    for d in range(1, n_ch):
        pltpu.make_async_remote_copy(
            src_ref=weight_block(ch_peer(d)),
            dst_ref=weight.at[group, half],
            send_sem=w_send,
            recv_sem=w_recv,
            device_id=(me, ch_peer(d)),
            device_id_type=MESH,
        ).start()

    for copy in loads[1:]:
        copy.wait()

    lane = lax.broadcasted_iota(jnp.int32, (1, chl), 1)

    def place(owner, c):
        return (c // 2) * wide_half + 2 * owner + c % 2

    def picked(row, c):
        return jnp.sum(jnp.where(lane == place(me, c), row, 0.0), axis=1, keepdims=True)

    pick_rows = lax.broadcasted_iota(jnp.int32, (8, chl), 0)
    pick_cols = lax.broadcasted_iota(jnp.int32, (8, chl), 1)
    pick = jnp.zeros((8, chl), F32)
    for r in range(8):
        here = (pick_rows == r) & (pick_cols == place(me - half + r // 4, r % 4))
        pick = jnp.where(here, 1.0, pick)

    hidden = mid.shape[1]
    turns = freq[pl.ds(half, 1), :] * (1.0 / (2.0 * math.pi))
    both = first[...].astype(F32)
    base = jnp.where(half == 0, both[:, 0, :], both[:, 1, :]) * turns
    shifts = bias[half] * turns - 0.25
    base = jnp.concatenate([base, shifts[0:1], jnp.zeros((8 - EMB - 1, hidden), F32)], axis=0)
    flip_h = eye(hidden, BF16)
    lift = dot_nt(flip_h, jnp.concatenate(terms(base, 3), axis=0).astype(BF16)).astype(BF16)
    mixed = terms(mid[half].astype(F32) * turns, 2)
    mixed = mixed + terms(shifts[1:2], 3) + [jnp.zeros((13, hidden), F32)]
    mix = dot_nt(flip_h, jnp.concatenate(mixed, axis=0).astype(BF16)).astype(BF16)
    pull = dot_nt(pick.astype(BF16), last[half]).astype(BF16)
    rate_row = jnp.where(pick > 0.0, decay[pl.ds(half, 1), :], 0.0)
    rate = jnp.sum(rate_row, axis=1, keepdims=True)
    gain = jnp.sqrt(2.0 * rate)
    ones = (lax.broadcasted_iota(jnp.int32, (16, chunk), 0) < 3).astype(F32).astype(BF16)

    def sine_of(t):
        e = 0.25 - jnp.abs(t - jnp.round(t))
        e2 = e * e
        acc = sine[-1]
        for term in sine[-2::-1]:
            acc = acc * e2 + term
        return (acc * e).astype(BF16)

    def filter_step(i, carry):
        start = pl.multiple_of(i * chunk, chunk)
        act_one = sine_of(dot(lift, feat[:, pl.ds(start, chunk)]))
        act_two = sine_of(dot(mix, jnp.concatenate([act_one, act_one, ones], axis=0)))
        raw = dot(pull, act_two)
        lag = (lax.broadcasted_iota(jnp.int32, (8, chunk), 1) + start).astype(F32)
        value = raw * jnp.exp(-rate * lag) * gain
        for q in range(chunk // LANES):
            row = pl.multiple_of((i * (chunk // LANES) + q) * 8, 8)
            filt[half, pl.ds(row, 8), :] = value[:, q * LANES : (q + 1) * LANES]
        return carry

    count = seq_len // chunk
    for part in range(2):
        lax.fori_loop(part * count // 2, (part + 1) * count // 2, filter_step, 0)
        done = filt.at[half, pl.ds(part * n_ctx * 4, n_ctx * 4)]
        pltpu.make_async_remote_copy(
            src_ref=done,
            dst_ref=done,
            send_sem=filt_send,
            recv_sem=filt_recv,
            device_id=(partner, group),
            device_id_type=MESH,
        ).start()

    tw_re, tw_im = twiddle[0], twiddle[1]

    def forward(parts):
        high = parts[0]
        part = dot(lead[0], high) + dot(lead[1], high)
        if len(parts) > 1:
            part = part + dot(lead[0], parts[1])
        rows = []
        for c in range(high.shape[1] // LANES):
            re = part[:kept, c * LANES : (c + 1) * LANES]
            im = part[kept:, c * LANES : (c + 1) * LANES]
            rows.append(jnp.concatenate([re * tw_re - im * tw_im, re * tw_im + im * tw_re], axis=1))
        high, low = halves(jnp.concatenate(rows, axis=0))
        return dot(high, wide[0]) + dot(low, wide[0]) + dot(high, wide[1])

    def inverse(spec):
        high, low = halves(spec)
        part = dot(high, wide[2]) + dot(low, wide[2]) + dot(high, wide[3])
        cols = []
        for c in range(spec.shape[0] // kept):
            re = part[c * kept : (c + 1) * kept, :LANES]
            im = part[c * kept : (c + 1) * kept, LANES:]
            cols.append(jnp.concatenate([re * tw_re + im * tw_im, im * tw_re - re * tw_im], axis=0))
        high, low = halves(jnp.concatenate(cols, axis=1))
        return dot(tail[0], high) + dot(tail[0], low) + dot(tail[1], high)

    def make_spectrum(o):
        cols = [filt[o, pl.ds(4 * half + c, n_ctx, stride=8), :] for c in range(4)]
        spectrum[o] = forward(halves(jnp.concatenate(cols, axis=1)))

    make_spectrum(half)
    sent = filt.at[half]
    pltpu.make_async_copy(sent, sent, filt_send).wait()
    came = filt.at[1 - half]
    pltpu.make_async_copy(came, came, filt_recv).wait()
    make_spectrum(1 - half)

    def convolve(o, h, state):
        spec = forward((state.astype(BF16),))
        re, im = spec[:, :LANES], spec[:, LANES:]
        rows = slice(2 * h * kept, 2 * (h + 1) * kept)
        f_re, f_im = spectrum[o, rows, :LANES], spectrum[o, rows, LANES:]
        return inverse(jnp.concatenate([re * f_re - im * f_im, re * f_im + im * f_re], axis=1))

    row0 = lax.broadcasted_iota(jnp.int32, (n_ctx, LANES), 0) == 0
    lane_at = lax.broadcasted_iota(jnp.int32, (n_ctx, LANES), 1)

    def delayed(x, by):
        near = pltpu.roll(x, by, 1)
        carried = jnp.where(row0, 0.0, pltpu.roll(near, 1, 0))
        return jnp.where(lane_at < by, carried, near)

    def shortened(h, s):
        signal[h, s] = incoming[h, :, s].astype(F32).reshape(n_ctx * 2, tok)
        cols = []
        for c in range(2):
            x = signal[h, s, pl.ds(c, n_ctx, stride=2), :]
            taps = [picked(short[s, i : i + 1, :], 2 * h + c) for i in range(3)]
            cols.append(taps[0] * x + taps[1] * delayed(x, 1) + taps[2] * delayed(x, 2))
        return jnp.concatenate(cols, axis=1).astype(BF16).astype(F32)

    for h in range(2):
        pltpu.make_async_copy(incoming.at[h], incoming.at[h], recv_sem.at[h]).wait()
        state = shortened(h, 0)
        for o in range(2):
            direct = jnp.concatenate(
                [jnp.broadcast_to(picked(skip[o : o + 1, :], 2 * h + c), (1, LANES)) for c in range(2)],
                axis=1,
            )
            output = convolve(o, h, state) + direct * state
            if o == 0:
                state = (shortened(h, 1) * output).astype(BF16).astype(F32)
        for c in range(2):
            signal[h, 0, pl.ds(c, n_ctx, stride=2), :] = output[:, c * LANES : (c + 1) * LANES]
        back_out[h] = signal[h, 0].reshape(n_ctx, 2, tok).astype(BF16)

        pltpu.make_async_copy(back_out.at[h, me], back_in.at[h, me], back_recv.at[h]).start()

        def send_back(peer):
            pltpu.make_async_remote_copy(
                src_ref=back_out.at[h, peer],
                dst_ref=back_in.at[h, me],
                send_sem=back_send.at[h],
                recv_sem=back_recv.at[h],
                device_id=(peer, group),
                device_id_type=MESH,
            ).start()

        for_ctx_peers(send_back)

    pltpu.make_async_copy(halo, halo, halo_recv).wait()
    near = streams[2].astype(F32)
    ahead = jnp.where(me > 0, halo[...].astype(F32), 0.0)
    at_row = lax.broadcasted_iota(jnp.int32, (tok, chl), 0)
    one = jnp.where(at_row == 0, ahead[7:8], pltpu.roll(near, 1, 0))
    two = jnp.where(at_row == 0, ahead[6:7], jnp.where(at_row == 1, ahead[7:8], pltpu.roll(near, 2, 0)))
    made = short[2, 0:1] * near + short[2, 1:2] * one + short[2, 2:3] * two
    gate[...] = made.astype(BF16).astype(F32)

    pltpu.make_async_copy(weight.at[:, half], weight.at[:, half], w_recv).wait()
    swap = pltpu.make_async_remote_copy(
        src_ref=weight.at[:, half],
        dst_ref=weight.at[:, half],
        send_sem=pair_send,
        recv_sem=pair_recv,
        device_id=(partner, group),
        device_id_type=MESH,
    )
    swap.start()

    for h in range(2):
        pltpu.make_async_copy(back_in.at[h], back_in.at[h], back_recv.at[h]).wait()
        block = back_in[h].astype(F32).reshape(n_ctx * 2, tok)
        turned = dot_nt(flip, block.astype(BF16))
        gathered[h, group] = (gate[:, h * wide_half : (h + 1) * wide_half] * turned).astype(BF16)
        for d in range(1, n_ch):
            pltpu.make_async_remote_copy(
                src_ref=gathered.at[h, group],
                dst_ref=gathered.at[h, group],
                send_sem=ring_send.at[h],
                recv_sem=ring_recv.at[h, group],
                device_id=(me, ch_peer(d)),
                device_id_type=MESH,
            ).start()

    swap.wait()

    total = jnp.zeros((tok, cols_out), F32)
    for h in range(2):
        for d in range(n_ch):
            peer = ch_peer(d)
            if d > 0:
                came = gathered.at[h, peer]
                pltpu.make_async_copy(came, came, ring_recv.at[h, peer]).wait()
            total = total + dot(gathered[h, peer], weight[peer, h])
    out_ref[...] = total.astype(BF16)

    for h in range(2):
        sent = outgoing.at[h, pl.ds(0, n_ctx - 1)]
        pltpu.make_async_copy(sent, sent, send_sem.at[h]).wait()
        sent = back_out.at[h, pl.ds(0, n_ctx - 1)]
        pltpu.make_async_copy(sent, sent, back_send.at[h]).wait()
        sent = gathered.at[h, pl.ds(0, n_ch - 1)]
        pltpu.make_async_copy(sent, sent, ring_send.at[h]).wait()
    pltpu.make_async_copy(halo, halo, halo_send).wait()
    sent = weight.at[pl.ds(0, n_ch - 1), half]
    pltpu.make_async_copy(sent, sent, w_send).wait()


def solution(mesh):
    n_ctx, n_ch = mesh.shape["ctx"], mesh.shape["ch"]

    def per_device(
        streams,
        short_weight,
        filt_first,
        filt_bias,
        filt_mid,
        filt_freq,
        filt_last,
        decay,
        skip,
        out_weight,
    ):
        tok, chl = streams.shape[1], streams.shape[2]
        seq_len = tok * n_ctx
        kept = (n_ctx + 1 + 7) // 8 * 8
        cols_out = out_weight.shape[1] // n_ch
        lead, tail, twiddle, wide = transform_tables(n_ctx, kept)
        feat = feature_table(seq_len)
        args = (
            streams,
            short_weight,
            jnp.transpose(filt_first, (1, 0, 2)),
            filt_bias,
            filt_mid,
            filt_freq,
            filt_last,
            decay,
            skip,
            out_weight,
            jnp.asarray(lead),
            jnp.asarray(tail),
            jnp.asarray(twiddle),
            jnp.asarray(wide),
            jnp.asarray(feat),
        )

        def vmem(x):
            return pltpu.VMEM(x.shape, x.dtype)

        staged = [vmem(args[i]) for i in (0, 1, 2, 3, 4, 5, 6, 7, 8, 10, 11, 12, 13, 14)]
        dma = pltpu.SemaphoreType.DMA
        return pl.pallas_call(
            functools.partial(kernel, n_ctx, n_ch, min(1024, seq_len // 2), sine_terms()),
            out_shape=pltpu.VMEM((tok, cols_out), BF16),
            in_specs=[pl.BlockSpec(memory_space=pl.ANY)] * len(args),
            out_specs=pl.BlockSpec(memory_space=pltpu.VMEM),
            scratch_shapes=staged
            + [
                pltpu.VMEM((2, n_ctx, 2, 2, tok), BF16),
                pltpu.VMEM((2, n_ctx, 2, 2, tok), BF16),
                pltpu.VMEM((2, 2, n_ctx * 2, tok), F32),
                pltpu.VMEM((2, n_ctx * 8, LANES), F32),
                pltpu.VMEM((2, 4 * kept, 2 * LANES), F32),
                pltpu.VMEM((2, n_ctx, 2, tok), BF16),
                pltpu.VMEM((2, n_ctx, 2, tok), BF16),
                pltpu.VMEM((2, n_ch, tok, chl // 2), BF16),
                pltpu.VMEM((n_ch, 2, chl // 2, cols_out), BF16),
                pltpu.VMEM((8, chl), BF16),
                pltpu.VMEM((tok, chl), F32),
                dma((14,)),
                dma((2,)),
                dma((2,)),
                dma((2,)),
                dma((2,)),
                dma((2,)),
                dma((2, n_ch)),
                dma,
                dma,
                dma,
                dma,
                dma,
                dma,
                dma,
                dma,
            ],
            compiler_params=pltpu.CompilerParams(collective_id=0, has_side_effects=True),
        )(*args)

    return jax.shard_map(
        per_device,
        mesh=mesh,
        in_specs=(
            P(None, "ctx", "ch"),
            P(None, None, "ch"),
            P(),
            P(),
            P(),
            P(),
            P(None, None, "ch"),
            P(None, "ch"),
            P(None, "ch"),
            P("ch", None),
        ),
        out_specs=P("ctx", "ch"),
        check_vma=False,
    )
```

```python
import functools
import math

import jax
import jax.numpy as jnp
import numpy as np
from jax import lax
from jax.experimental import pallas as pl
from jax.experimental.pallas import tpu as pltpu
from jax.sharding import PartitionSpec as P

MESH = pl.DeviceIdType.MESH
BF16 = jnp.bfloat16
F32 = jnp.float32
EMB = 5
LANES = 128


def split_table(table):
    high = table.astype(np.float32).astype(jnp.bfloat16)
    low = (table - high.astype(np.float64)).astype(np.float32).astype(jnp.bfloat16)
    return np.stack([high, low])


def transform_tables(rows, kept):
    total = 2 * rows * LANES
    k = np.arange(kept)[:, None]
    live = k <= rows
    a = np.arange(rows)[None, :]
    b = np.arange(LANES)[None, :]
    angle = 2.0 * np.pi * ((k * a) % (2 * rows)) / (2 * rows)
    cos_a = np.where(live, np.cos(angle), 0.0)
    sin_a = np.where(live, np.sin(angle), 0.0)
    first = np.concatenate([cos_a, -sin_a], axis=0)
    weight = np.where((k == 0) | (k == rows), 1.0, 2.0) / total
    last = np.concatenate([(weight * cos_a).T, (-weight * sin_a).T], axis=1)
    turn = 2.0 * np.pi * ((k * b) % total) / total
    twiddle = np.stack([np.cos(turn), -np.sin(turn)]).astype(np.float32)
    j = np.arange(LANES)[:, None]
    phase = 2.0 * np.pi * ((j * b) % LANES) / LANES
    cos_b, sin_b = np.cos(phase), np.sin(phase)
    forward = np.block([[cos_b, -sin_b], [sin_b, cos_b]])
    wide = np.concatenate([split_table(forward), split_table(forward.T)])
    return split_table(first), split_table(last), twiddle, wide


def feature_table(seq_len):
    positions = np.arange(seq_len, dtype=np.int32)
    rows = [positions.astype(np.float32) / np.float32(seq_len)]
    cosines, sines = [], []
    for band in range((EMB - 1) // 2):
        wrapped = (band + 1) * positions % seq_len
        angle = np.float32(2.0 * math.pi / seq_len) * wrapped.astype(np.float32)
        cosines.append(np.cos(angle))
        sines.append(np.sin(angle))
    table = np.zeros((8, seq_len), np.float32)
    table[:EMB] = np.stack(rows + cosines + sines)
    table[EMB] = 1.0
    return np.concatenate([table] * 3).astype(jnp.bfloat16)


def sine_terms():
    e = 0.25 * np.cos(np.pi * (np.arange(400) + 0.5) / 800)
    basis = np.stack([e ** (2 * i + 1) for i in range(4)], axis=1)
    scale = 1.0 / np.maximum(np.abs(np.sin(2 * np.pi * e)), 1e-3)
    terms = np.linalg.lstsq(basis * scale[:, None], np.sin(2 * np.pi * e) * scale, rcond=None)[0]
    return [float(np.float32(t)) for t in terms]


def dot(a, b):
    return jnp.dot(a, b, preferred_element_type=F32)


def dot_nt(a, b):
    return lax.dot_general(a, b, (((1,), (1,)), ((), ())), preferred_element_type=F32)


def two_rows(a, b):
    both = dot(a, b)
    rows = a.shape[0] // 2
    return both[:rows] + both[rows:]


def halves(x):
    high = x.astype(BF16)
    return high, (x - high.astype(F32)).astype(BF16)


def eye(n, dtype):
    rows = lax.broadcasted_iota(jnp.int32, (n, n), 0)
    cols = lax.broadcasted_iota(jnp.int32, (n, n), 1)
    return (rows == cols).astype(F32).astype(dtype)


def terms(x, count):
    parts = []
    for _ in range(count):
        part = x.astype(BF16).astype(F32)
        parts.append(part)
        x = x - part
    return parts


def kernel(
    n_ctx,
    n_ch,
    chunk,
    sine,
    streams_in,
    short_in,
    first_in,
    bias_in,
    mid_in,
    freq_in,
    last_in,
    decay_in,
    skip_in,
    weight_in,
    lead_in,
    tail_in,
    twiddle_in,
    wide_in,
    feat_in,
    out_ref,
    streams,
    short,
    first,
    bias,
    mid,
    freq,
    last,
    decay,
    skip,
    lead,
    tail,
    twiddle,
    wide,
    feat,
    outgoing,
    incoming,
    signal,
    filt,
    spectrum,
    back_out,
    back_in,
    gathered,
    weight,
    halo,
    gate,
    load_sem,
    send_sem,
    recv_sem,
    back_send,
    back_recv,
    ring_send,
    ring_recv,
    w_send,
    w_recv,
    pair_send,
    pair_recv,
    filt_send,
    filt_recv,
    halo_send,
    halo_recv,
):
    me = lax.axis_index("ctx")
    group = lax.axis_index("ch")
    half = lax.rem(me, 2)
    partner = me + 1 - 2 * half
    tok, chl = streams.shape[1], streams.shape[2]
    wide_half = chl // 2
    kept = twiddle.shape[1]
    seq_len = feat.shape[1]

    def ctx_peer(d):
        return lax.rem(me + d, n_ctx)

    def ch_peer(d):
        return lax.rem(group + d, n_ch)

    n_y = n_ch // 2
    ring = [(dy, dx) for dy in range(n_y) for dx in range(2) if dy or dx]
    ring.sort(key=lambda p: min(p[0], n_y - p[0]) + 2 * p[1])

    def ring_peer(step):
        dy, dx = step
        return lax.rem(group // 2 + dy, n_y) * 2 + lax.rem(group + dx, 2)

    my_z = lax.rem(me, n_ctx // 2) // 2

    n_z = n_ctx // 4
    my_x = me // (2 * n_z)

    def device_at(x, z, core):
        return x * (2 * n_z) + 2 * z + core

    def block_at(x, z, core):
        return lax.rem(z + n_z // 4, n_z) * 4 + 2 * x + core

    mine = block_at(my_x, my_z, half)
    my_class = mine // (n_ctx // 2)

    def for_plane(z, act):
        act(1 - my_x, z, 1 - half)
        act(1 - my_x, z, half)
        act(my_x, z, 1 - half)

    def weight_peer(d):
        return (ctx_peer(n_ctx // 2) if d % 2 else me, ch_peer(d))

    def for_ctx_peers(act):
        quarter = n_ctx // 4
        act(ctx_peer(quarter))
        act(ctx_peer(3 * quarter))

        def step(e, carry):
            act(ctx_peer(quarter + e))
            act(ctx_peer(quarter - e))
            act(ctx_peer(3 * quarter + e))
            act(ctx_peer(3 * quarter - e))
            return carry

        lax.fori_loop(1, quarter, step, 0)
        act(ctx_peer(2 * quarter))

    loads = []
    pairs = (
        (streams_in, streams),
        (feat_in, feat),
        (first_in, first),
        (bias_in, bias),
        (mid_in, mid),
        (freq_in, freq),
        (last_in, last),
        (decay_in, decay),
        (lead_in, lead),
        (twiddle_in, twiddle),
        (wide_in, wide),
        (short_in, short),
        (skip_in, skip),
        (tail_in, tail),
    )
    for i, (src, dst) in enumerate(pairs):
        copy = pltpu.make_async_copy(src, dst, load_sem.at[i])
        copy.start()
        loads.append(copy)

    barrier = pltpu.get_barrier_semaphore()

    def greet_ctx(peer):
        pl.semaphore_signal(barrier, inc=1, device_id=(peer, group), device_id_type=MESH)

    for_ctx_peers(greet_ctx)
    for d in range(1, n_ch):
        pl.semaphore_signal(barrier, inc=1, device_id=(me, ch_peer(d)), device_id_type=MESH)
        if d % 2:
            pl.semaphore_signal(barrier, inc=1, device_id=weight_peer(d), device_id_type=MESH)

    loads[0].wait()
    flip = eye(tok, BF16)
    turner = eye(chl, BF16)
    for s in range(2):
        turned = dot_nt(turner, streams[s])
        outgoing[:, s] = turned.reshape(n_ctx, 4, tok).astype(BF16)

    lane = lax.broadcasted_iota(jnp.int32, (1, chl), 1)

    def picked(row, c):
        return jnp.sum(jnp.where(lane == 4 * mine + c, row, 0.0), axis=1, keepdims=True)

    def forward(parts):
        high = parts[0]
        part = two_rows(lead[...].reshape(4 * kept, n_ctx), high)
        if len(parts) > 1:
            part = part + dot(lead[0], parts[1])
        rows = []
        for c in range(high.shape[1] // LANES):
            re = part[:kept, c * LANES : (c + 1) * LANES]
            im = part[kept:, c * LANES : (c + 1) * LANES]
            rows.append(jnp.concatenate([re * twiddle[0] - im * twiddle[1], re * twiddle[1] + im * twiddle[0]], axis=1))
        high, low = halves(jnp.concatenate(rows, axis=0))
        return two_rows(jnp.concatenate([high, low], axis=0), wide[0]) + dot(high, wide[1])

    def inverse(spec):
        high, low = halves(spec)
        part = two_rows(jnp.concatenate([high, low], axis=0), wide[2]) + dot(high, wide[3])
        cols = []
        for c in range(spec.shape[0] // kept):
            re = part[c * kept : (c + 1) * kept, :LANES]
            im = part[c * kept : (c + 1) * kept, LANES:]
            cols.append(jnp.concatenate([re * twiddle[0] + im * twiddle[1], im * twiddle[0] - re * twiddle[1]], axis=0))
        high, low = halves(jnp.concatenate(cols, axis=1))
        return two_rows(tail[...].reshape(2 * n_ctx, 2 * kept), high) + dot(tail[0], low)

    def make_spectrum(o):
        cols = [filt[o, pl.ds(4 * half + c, n_ctx, stride=8), :] for c in range(4)]
        spectrum[o] = forward(halves(jnp.concatenate(cols, axis=1)))

    def pass_filter(part, parts):
        rows = n_ctx * 8 // parts
        done = filt.at[half, pl.ds(part * rows, rows)]
        pltpu.make_async_remote_copy(
            src_ref=done,
            dst_ref=done,
            send_sem=filt_send,
            recv_sem=filt_recv,
            device_id=(partner, group),
            device_id_type=MESH,
        ).start()

    def make_filter(pass_on):
        for copy in loads[1:]:
            copy.wait()
        pick_rows = lax.broadcasted_iota(jnp.int32, (8, chl), 0)
        pick_cols = lax.broadcasted_iota(jnp.int32, (8, chl), 1)
        pick = jnp.zeros((8, chl), F32)
        for r in range(8):
            here = (pick_rows == r) & (pick_cols == 4 * (mine - half) + r)
            pick = jnp.where(here, 1.0, pick)

        hidden = mid.shape[1]
        turns = freq[pl.ds(half, 1), :] * (1.0 / (2.0 * math.pi))
        both = first[...].astype(F32)
        base = jnp.where(half == 0, both[:, 0, :], both[:, 1, :]) * turns
        shifts = bias[half] * turns - 0.25
        base = jnp.concatenate([base, shifts[0:1], jnp.zeros((8 - EMB - 1, hidden), F32)], axis=0)
        flip_h = eye(hidden, BF16)
        lift = dot_nt(flip_h, jnp.concatenate(terms(base, 3), axis=0).astype(BF16)).astype(BF16)
        mixed = terms(mid[half].astype(F32) * turns, 2)
        mixed = mixed + terms(shifts[1:2], 3) + [jnp.zeros((13, hidden), F32)]
        mix = dot_nt(flip_h, jnp.concatenate(mixed, axis=0).astype(BF16)).astype(BF16)
        pull = dot_nt(pick.astype(BF16), last[half]).astype(BF16)
        rate_row = jnp.where(pick > 0.0, decay[pl.ds(half, 1), :], 0.0)
        rate = jnp.sum(rate_row, axis=1, keepdims=True)
        gain = jnp.sqrt(2.0 * rate)
        ones = (lax.broadcasted_iota(jnp.int32, (16, chunk), 0) < 3).astype(F32).astype(BF16)

        def sine_of(t):
            e = 0.25 - jnp.abs(t - jnp.round(t))
            e2 = e * e
            acc = sine[-1]
            for term in sine[-2::-1]:
                acc = acc * e2 + term
            return (acc * e).astype(BF16)

        def filter_step(i, carry):
            start = pl.multiple_of(i * chunk, chunk)
            act_one = sine_of(dot(lift, feat[:, pl.ds(start, chunk)]))
            act_two = sine_of(dot(mix, jnp.concatenate([act_one, act_one, ones], axis=0)))
            raw = dot(pull, act_two)
            lag = (lax.broadcasted_iota(jnp.int32, (8, chunk), 1) + start).astype(F32)
            value = raw * jnp.exp(-rate * lag) * gain
            for q in range(chunk // LANES):
                row = pl.multiple_of((i * (chunk // LANES) + q) * 8, 8)
                filt[half, pl.ds(row, 8), :] = value[:, q * LANES : (q + 1) * LANES]
            return carry

        count = seq_len // chunk
        for part in range(2):
            lax.fori_loop(part * count // 2, (part + 1) * count // 2, filter_step, 0)
            if pass_on:
                pass_filter(part, 2)
        make_spectrum(half)

    early = my_z < n_ctx // 8

    pl.when(early)(functools.partial(make_filter, False))

    pl.semaphore_wait(barrier, n_ctx + n_ch - 2 + n_ch // 2)

    pltpu.make_async_copy(outgoing.at[mine], incoming.at[me], recv_sem).start()

    def send(x, z, core):
        pltpu.make_async_remote_copy(
            src_ref=outgoing.at[block_at(x, z, core)],
            dst_ref=incoming.at[me],
            send_sem=send_sem,
            recv_sem=recv_sem,
            device_id=(device_at(x, z, core), group),
            device_id_type=MESH,
        ).start()

    def send_far(e, carry):
        for off in (n_z // 2 - e, n_z // 2 + e):
            z = lax.rem(my_z + off, n_z)
            for_plane(z, send)
            send(my_x, z, half)
        return carry

    opposite = lax.rem(my_z + n_z // 2, n_z)
    for_plane(opposite, send)
    send(my_x, opposite, half)
    lax.fori_loop(1, n_z // 2, send_far, 0)
    for_plane(my_z, send)

    pltpu.make_async_remote_copy(
        src_ref=streams.at[2, pl.ds(tok - 8, 8)],
        dst_ref=halo,
        send_sem=halo_send,
        recv_sem=halo_recv,
        device_id=(ctx_peer(1), group),
        device_id_type=MESH,
    ).start()

    depth, cols_out = weight.shape[2], weight.shape[3]

    def weight_block(g):
        return weight_in.at[
            pl.ds(pl.multiple_of(half * depth, depth), depth),
            pl.ds(pl.multiple_of(g * cols_out, cols_out), cols_out),
        ]

    pltpu.make_async_copy(weight_block(group), weight.at[group, half], w_recv).start()
    for d in range(1, n_ch):
        pltpu.make_async_remote_copy(
            src_ref=weight_block(ch_peer(d)),
            dst_ref=weight.at[group, half],
            send_sem=w_send,
            recv_sem=w_recv,
            device_id=weight_peer(d),
            device_id_type=MESH,
        ).start()

    pl.when(early)(functools.partial(pass_filter, 0, 1))
    pl.when(jnp.logical_not(early))(functools.partial(make_filter, True))

    sent = filt.at[half]
    pltpu.make_async_copy(sent, sent, filt_send).wait()
    came = filt.at[1 - half]
    pltpu.make_async_copy(came, came, filt_recv).wait()
    make_spectrum(1 - half)

    def convolve(o, state):
        spec = forward((state.astype(BF16),))
        re, im = spec[:, :LANES], spec[:, LANES:]
        f_re, f_im = spectrum[o, :, :LANES], spectrum[o, :, LANES:]
        return inverse(jnp.concatenate([re * f_re - im * f_im, re * f_im + im * f_re], axis=1))

    row0 = lax.broadcasted_iota(jnp.int32, (n_ctx, LANES), 0) == 0
    lane_at = lax.broadcasted_iota(jnp.int32, (n_ctx, LANES), 1)

    def delayed(x, by):
        near = pltpu.roll(x, by, 1)
        carried = jnp.where(row0, 0.0, pltpu.roll(near, 1, 0))
        return jnp.where(lane_at < by, carried, near)

    def shortened(s):
        signal[s] = incoming[:, s].astype(F32).reshape(n_ctx * 4, tok)
        cols = []
        for c in range(4):
            x = signal[s, pl.ds(c, n_ctx, stride=4), :]
            taps = [picked(short[s, i : i + 1, :], c) for i in range(3)]
            cols.append(taps[0] * x + taps[1] * delayed(x, 1) + taps[2] * delayed(x, 2))
        return jnp.concatenate(cols, axis=1).astype(BF16).astype(F32)

    pltpu.make_async_copy(incoming, incoming, recv_sem).wait()
    state = shortened(0)
    for o in range(2):
        direct = jnp.concatenate(
            [jnp.broadcast_to(picked(skip[o : o + 1, :], c), (1, LANES)) for c in range(4)], axis=1
        )
        output = convolve(o, state) + direct * state
        if o == 0:
            state = (shortened(1) * output).astype(BF16).astype(F32)
    for c in range(4):
        signal[0, pl.ds(c, n_ctx, stride=4), :] = output[:, c * LANES : (c + 1) * LANES]
    back_out[...] = signal[0].reshape(n_ctx, 4, tok).astype(BF16)

    landing = back_in.at[my_class, lax.rem(mine, n_ctx // 2)]
    pltpu.make_async_copy(back_out.at[me], landing, back_recv.at[my_class]).start()

    def send_back(x, z, core):
        place = device_at(x, z, core)
        pltpu.make_async_remote_copy(
            src_ref=back_out.at[place],
            dst_ref=landing,
            send_sem=back_send,
            recv_sem=back_recv.at[my_class],
            device_id=(place, group),
            device_id_type=MESH,
        ).start()

    def send_plane(z, carry):
        for_plane(z, send_back)

        @pl.when(z != my_z)
        def _():
            send_back(my_x, z, half)

        return carry

    lax.fori_loop(0, n_z, send_plane, 0)

    pltpu.make_async_copy(halo, halo, halo_recv).wait()
    near = streams[2].astype(F32)
    ahead = jnp.where(me > 0, halo[...].astype(F32), 0.0)
    at_row = lax.broadcasted_iota(jnp.int32, (tok, chl), 0)
    one = jnp.where(at_row == 0, ahead[7:8], pltpu.roll(near, 1, 0))
    two = jnp.where(at_row == 0, ahead[6:7], jnp.where(at_row == 1, ahead[7:8], pltpu.roll(near, 2, 0)))
    made = short[2, 0:1] * near + short[2, 1:2] * one + short[2, 2:3] * two
    gate[...] = made.astype(BF16).astype(F32)

    for h in range(2):
        pltpu.make_async_copy(back_in.at[h], back_in.at[h], back_recv.at[h]).wait()
        block = back_in[h].astype(F32).reshape(wide_half, tok)
        turned = dot_nt(flip, block.astype(BF16))
        gathered[h, group] = (gate[:, h * wide_half : (h + 1) * wide_half] * turned).astype(BF16)
        for hop in ring[::-1]:
            pltpu.make_async_remote_copy(
                src_ref=gathered.at[h, group],
                dst_ref=gathered.at[h, group],
                send_sem=ring_send.at[h],
                recv_sem=ring_recv.at[h, group],
                device_id=(me, ring_peer(hop)),
                device_id_type=MESH,
            ).start()
        if h == 0:
            pltpu.make_async_copy(weight.at[:, half], weight.at[:, half], w_recv).wait()
            swap = pltpu.make_async_remote_copy(
                src_ref=weight.at[:, half],
                dst_ref=weight.at[:, half],
                send_sem=pair_send,
                recv_sem=pair_recv,
                device_id=(partner, group),
                device_id_type=MESH,
            )
            swap.start()

    swap.wait()

    total = jnp.zeros((tok, cols_out), F32)
    for h in range(2):
        for hop in [(0, 0)] + ring:
            peer = ring_peer(hop)
            if hop != (0, 0):
                came = gathered.at[h, peer]
                pltpu.make_async_copy(came, came, ring_recv.at[h, peer]).wait()
            total = total + dot(gathered[h, peer], weight[peer, h])
    out_ref[...] = total.astype(BF16)

    sent = outgoing.at[pl.ds(0, n_ctx - 1)]
    pltpu.make_async_copy(sent, sent, send_sem).wait()
    sent = back_out.at[pl.ds(0, n_ctx - 1)]
    pltpu.make_async_copy(sent, sent, back_send).wait()
    for h in range(2):
        sent = gathered.at[h, pl.ds(0, n_ch - 1)]
        pltpu.make_async_copy(sent, sent, ring_send.at[h]).wait()
    pltpu.make_async_copy(halo, halo, halo_send).wait()
    sent = weight.at[pl.ds(0, n_ch - 1), half]
    pltpu.make_async_copy(sent, sent, w_send).wait()


def solution(mesh):
    n_ctx, n_ch = mesh.shape["ctx"], mesh.shape["ch"]

    def per_device(
        streams,
        short_weight,
        filt_first,
        filt_bias,
        filt_mid,
        filt_freq,
        filt_last,
        decay,
        skip,
        out_weight,
    ):
        tok, chl = streams.shape[1], streams.shape[2]
        seq_len = tok * n_ctx
        kept = (n_ctx + 1 + 7) // 8 * 8
        cols_out = out_weight.shape[1] // n_ch
        lead, tail, twiddle, wide = transform_tables(n_ctx, kept)
        feat = feature_table(seq_len)
        args = (
            streams,
            short_weight,
            jnp.transpose(filt_first, (1, 0, 2)),
            filt_bias,
            filt_mid,
            filt_freq,
            filt_last,
            decay,
            skip,
            out_weight,
            jnp.asarray(lead),
            jnp.asarray(tail),
            jnp.asarray(twiddle),
            jnp.asarray(wide),
            jnp.asarray(feat),
        )

        def vmem(x):
            return pltpu.VMEM(x.shape, x.dtype)

        staged = [vmem(args[i]) for i in (0, 1, 2, 3, 4, 5, 6, 7, 8, 10, 11, 12, 13, 14)]
        dma = pltpu.SemaphoreType.DMA
        return pl.pallas_call(
            functools.partial(kernel, n_ctx, n_ch, min(1024, seq_len // 2), sine_terms()),
            out_shape=pltpu.VMEM((tok, cols_out), BF16),
            in_specs=[pl.BlockSpec(memory_space=pl.ANY)] * len(args),
            out_specs=pl.BlockSpec(memory_space=pltpu.VMEM),
            scratch_shapes=staged
            + [
                pltpu.VMEM((n_ctx, 2, 4, tok), BF16),
                pltpu.VMEM((n_ctx, 2, 4, tok), BF16),
                pltpu.VMEM((2, n_ctx * 4, tok), F32),
                pltpu.VMEM((2, n_ctx * 8, LANES), F32),
                pltpu.VMEM((2, 4 * kept, 2 * LANES), F32),
                pltpu.VMEM((n_ctx, 4, tok), BF16),
                pltpu.VMEM((2, n_ctx // 2, 4, tok), BF16),
                pltpu.VMEM((2, n_ch, tok, chl // 2), BF16),
                pltpu.VMEM((n_ch, 2, chl // 2, cols_out), BF16),
                pltpu.VMEM((8, chl), BF16),
                pltpu.VMEM((tok, chl), F32),
                dma((14,)),
                dma,
                dma,
                dma,
                dma((2,)),
                dma((2,)),
                dma((2, n_ch)),
                dma,
                dma,
                dma,
                dma,
                dma,
                dma,
                dma,
                dma,
            ],
            compiler_params=pltpu.CompilerParams(collective_id=0, has_side_effects=True),
        )(*args)

    return jax.shard_map(
        per_device,
        mesh=mesh,
        in_specs=(
            P(None, "ctx", "ch"),
            P(None, None, "ch"),
            P(),
            P(),
            P(),
            P(),
            P(None, None, "ch"),
            P(None, "ch"),
            P(None, "ch"),
            P("ch", None),
        ),
        out_specs=P("ctx", "ch"),
        check_vma=False,
    )
```

```python
import functools
import math

import jax
import jax.numpy as jnp
import numpy as np
from jax import lax
from jax.experimental import pallas as pl
from jax.experimental.pallas import tpu as pltpu
from jax.sharding import PartitionSpec as P

MESH = pl.DeviceIdType.MESH
BF16 = jnp.bfloat16
F32 = jnp.float32
EMB = 5
LANES = 128


def split_table(table):
    high = table.astype(np.float32).astype(jnp.bfloat16)
    low = (table - high.astype(np.float64)).astype(np.float32).astype(jnp.bfloat16)
    return np.stack([high, low])


def transform_tables(rows, kept):
    total = 2 * rows * LANES
    k = np.arange(kept)[:, None]
    live = k <= rows
    a = np.arange(rows)[None, :]
    b = np.arange(LANES)[None, :]
    angle = 2.0 * np.pi * ((k * a) % (2 * rows)) / (2 * rows)
    cos_a = np.where(live, np.cos(angle), 0.0)
    sin_a = np.where(live, np.sin(angle), 0.0)
    first = np.concatenate([cos_a, -sin_a], axis=0)
    weight = np.where((k == 0) | (k == rows), 1.0, 2.0) / total
    last = np.concatenate([(weight * cos_a).T, (-weight * sin_a).T], axis=1)
    turn = 2.0 * np.pi * ((k * b) % total) / total
    twiddle = np.stack([np.cos(turn), -np.sin(turn)]).astype(np.float32)
    j = np.arange(LANES)[:, None]
    phase = 2.0 * np.pi * ((j * b) % LANES) / LANES
    cos_b, sin_b = np.cos(phase), np.sin(phase)
    forward = np.block([[cos_b, -sin_b], [sin_b, cos_b]])
    wide = np.concatenate([split_table(forward), split_table(forward.T)])
    return split_table(first), split_table(last), twiddle, wide


def feature_table(seq_len):
    positions = np.arange(seq_len, dtype=np.int32)
    rows = [positions.astype(np.float32) / np.float32(seq_len)]
    cosines, sines = [], []
    for band in range((EMB - 1) // 2):
        wrapped = (band + 1) * positions % seq_len
        angle = np.float32(2.0 * math.pi / seq_len) * wrapped.astype(np.float32)
        cosines.append(np.cos(angle))
        sines.append(np.sin(angle))
    table = np.zeros((8, seq_len), np.float32)
    table[:EMB] = np.stack(rows + cosines + sines)
    table[EMB] = 1.0
    return np.concatenate([table] * 3).astype(jnp.bfloat16)


def sine_terms():
    e = 0.25 * np.cos(np.pi * (np.arange(400) + 0.5) / 800)
    basis = np.stack([e ** (2 * i + 1) for i in range(4)], axis=1)
    scale = 1.0 / np.maximum(np.abs(np.sin(2 * np.pi * e)), 1e-3)
    terms = np.linalg.lstsq(basis * scale[:, None], np.sin(2 * np.pi * e) * scale, rcond=None)[0]
    return [float(np.float32(t)) for t in terms]


def dot(a, b):
    return jnp.dot(a, b, preferred_element_type=F32)


def dot_nt(a, b):
    return lax.dot_general(a, b, (((1,), (1,)), ((), ())), preferred_element_type=F32)


def two_rows(a, b):
    both = dot(a, b)
    rows = a.shape[0] // 2
    return both[:rows] + both[rows:]


def halves(x):
    high = x.astype(BF16)
    return high, (x - high.astype(F32)).astype(BF16)


def eye(n, dtype):
    rows = lax.broadcasted_iota(jnp.int32, (n, n), 0)
    cols = lax.broadcasted_iota(jnp.int32, (n, n), 1)
    return (rows == cols).astype(F32).astype(dtype)


def terms(x, count):
    parts = []
    for _ in range(count):
        part = x.astype(BF16).astype(F32)
        parts.append(part)
        x = x - part
    return parts


def kernel(
    n_ctx,
    n_ch,
    chunk,
    sine,
    streams_in,
    short_in,
    first_in,
    bias_in,
    mid_in,
    freq_in,
    last_in,
    decay_in,
    skip_in,
    weight_in,
    lead_in,
    tail_in,
    twiddle_in,
    wide_in,
    feat_in,
    out_ref,
    streams,
    short,
    first,
    bias,
    mid,
    freq,
    last,
    decay,
    skip,
    lead,
    tail,
    twiddle,
    wide,
    feat,
    outgoing,
    incoming,
    signal,
    filt,
    spectrum,
    back_out,
    back_in,
    gathered,
    weight,
    halo,
    gate,
    load_sem,
    send_sem,
    recv_sem,
    back_send,
    back_recv,
    ring_send,
    ring_recv,
    w_send,
    w_recv,
    pair_send,
    pair_recv,
    filt_send,
    filt_recv,
    halo_send,
    halo_recv,
):
    me = lax.axis_index("ctx")
    group = lax.axis_index("ch")
    half = lax.rem(me, 2)
    partner = me + 1 - 2 * half
    tok, chl = streams.shape[1], streams.shape[2]
    wide_half = chl // 2
    kept = twiddle.shape[1]
    seq_len = feat.shape[1]

    def ctx_peer(d):
        return lax.rem(me + d, n_ctx)

    def ch_peer(d):
        return lax.rem(group + d, n_ch)

    n_y = n_ch // 2
    ring = [(dy, dx) for dy in range(n_y) for dx in range(2) if dy or dx]
    ring.sort(key=lambda p: min(p[0], n_y - p[0]) + 2 * p[1])

    def ring_peer(step):
        dy, dx = step
        return lax.rem(group // 2 + dy, n_y) * 2 + lax.rem(group + dx, 2)

    my_z = lax.rem(me, n_ctx // 2) // 2

    n_z = n_ctx // 4
    my_x = me // (2 * n_z)

    def device_at(x, z, core):
        return x * (2 * n_z) + 2 * z + core

    def block_at(x, z, core):
        far_side = z // (n_z // 2)
        fold = z + far_side * (n_z - 1 - 2 * z)
        return (2 * fold + far_side) * 4 + 2 * x + core

    mine = block_at(my_x, my_z, half)
    n_class = back_in.shape[0]
    class_rows = chl // n_class
    my_class = mine // (n_ctx // n_class)

    def for_plane(z, act):
        act(1 - my_x, z, 1 - half)
        act(1 - my_x, z, half)
        act(my_x, z, 1 - half)

    def weight_peer(d):
        return (ctx_peer(n_ctx // 2) if d % 2 else me, ch_peer(d))

    def for_ctx_peers(act):
        quarter = n_ctx // 4
        act(ctx_peer(quarter))
        act(ctx_peer(3 * quarter))

        def step(e, carry):
            act(ctx_peer(quarter + e))
            act(ctx_peer(quarter - e))
            act(ctx_peer(3 * quarter + e))
            act(ctx_peer(3 * quarter - e))
            return carry

        lax.fori_loop(1, quarter, step, 0)
        act(ctx_peer(2 * quarter))

    loads = []
    pairs = (
        (streams_in, streams),
        (feat_in, feat),
        (first_in, first),
        (bias_in, bias),
        (mid_in, mid),
        (freq_in, freq),
        (last_in, last),
        (decay_in, decay),
        (lead_in, lead),
        (twiddle_in, twiddle),
        (wide_in, wide),
        (short_in, short),
        (skip_in, skip),
        (tail_in, tail),
    )
    for i, (src, dst) in enumerate(pairs):
        copy = pltpu.make_async_copy(src, dst, load_sem.at[i])
        copy.start()
        loads.append(copy)

    barrier = pltpu.get_barrier_semaphore()

    def greet_ctx(peer):
        pl.semaphore_signal(barrier, inc=1, device_id=(peer, group), device_id_type=MESH)

    for_ctx_peers(greet_ctx)
    for d in range(1, n_ch):
        pl.semaphore_signal(barrier, inc=1, device_id=(me, ch_peer(d)), device_id_type=MESH)
        if d % 2:
            pl.semaphore_signal(barrier, inc=1, device_id=weight_peer(d), device_id_type=MESH)

    loads[0].wait()
    flip = eye(tok, BF16)
    turner = eye(chl, BF16)
    for s in range(2):
        turned = dot_nt(turner, streams[s])
        outgoing[:, s] = turned.reshape(n_ctx, 4, tok).astype(BF16)

    lane = lax.broadcasted_iota(jnp.int32, (1, chl), 1)

    def picked(row, c):
        return jnp.sum(jnp.where(lane == 4 * mine + c, row, 0.0), axis=1, keepdims=True)

    def forward(parts):
        high = parts[0]
        part = two_rows(lead[...].reshape(4 * kept, n_ctx), high)
        if len(parts) > 1:
            part = part + dot(lead[0], parts[1])
        rows = []
        for c in range(high.shape[1] // LANES):
            re = part[:kept, c * LANES : (c + 1) * LANES]
            im = part[kept:, c * LANES : (c + 1) * LANES]
            rows.append(jnp.concatenate([re * twiddle[0] - im * twiddle[1], re * twiddle[1] + im * twiddle[0]], axis=1))
        high, low = halves(jnp.concatenate(rows, axis=0))
        return two_rows(jnp.concatenate([high, low], axis=0), wide[0]) + dot(high, wide[1])

    def inverse(spec):
        high, low = halves(spec)
        part = two_rows(jnp.concatenate([high, low], axis=0), wide[2]) + dot(high, wide[3])
        cols = []
        for c in range(spec.shape[0] // kept):
            re = part[c * kept : (c + 1) * kept, :LANES]
            im = part[c * kept : (c + 1) * kept, LANES:]
            cols.append(jnp.concatenate([re * twiddle[0] + im * twiddle[1], im * twiddle[0] - re * twiddle[1]], axis=0))
        high, low = halves(jnp.concatenate(cols, axis=1))
        return two_rows(tail[...].reshape(2 * n_ctx, 2 * kept), high) + dot(tail[0], low)

    def make_spectrum(o):
        cols = [filt[o, pl.ds(4 * half + c, n_ctx, stride=8), :] for c in range(4)]
        spectrum[o] = forward(halves(jnp.concatenate(cols, axis=1)))

    def pass_filter(part, parts):
        rows = n_ctx * 8 // parts
        done = filt.at[half, pl.ds(part * rows, rows)]
        pltpu.make_async_remote_copy(
            src_ref=done,
            dst_ref=done,
            send_sem=filt_send,
            recv_sem=filt_recv,
            device_id=(partner, group),
            device_id_type=MESH,
        ).start()

    def make_filter(pass_on):
        for copy in loads[1:]:
            copy.wait()
        pick_rows = lax.broadcasted_iota(jnp.int32, (8, chl), 0)
        pick_cols = lax.broadcasted_iota(jnp.int32, (8, chl), 1)
        pick = jnp.zeros((8, chl), F32)
        for r in range(8):
            here = (pick_rows == r) & (pick_cols == 4 * (mine - half) + r)
            pick = jnp.where(here, 1.0, pick)

        hidden = mid.shape[1]
        turns = freq[pl.ds(half, 1), :] * (1.0 / (2.0 * math.pi))
        both = first[...].astype(F32)
        base = jnp.where(half == 0, both[:, 0, :], both[:, 1, :]) * turns
        shifts = bias[half] * turns - 0.25
        base = jnp.concatenate([base, shifts[0:1], jnp.zeros((8 - EMB - 1, hidden), F32)], axis=0)
        flip_h = eye(hidden, BF16)
        lift = dot_nt(flip_h, jnp.concatenate(terms(base, 3), axis=0).astype(BF16)).astype(BF16)
        mixed = terms(mid[half].astype(F32) * turns, 2)
        mixed = mixed + terms(shifts[1:2], 3) + [jnp.zeros((13, hidden), F32)]
        mix = dot_nt(flip_h, jnp.concatenate(mixed, axis=0).astype(BF16)).astype(BF16)
        pull = dot_nt(pick.astype(BF16), last[half]).astype(BF16)
        rate_row = jnp.where(pick > 0.0, decay[pl.ds(half, 1), :], 0.0)
        rate = jnp.sum(rate_row, axis=1, keepdims=True)
        gain = jnp.sqrt(2.0 * rate)
        ones = (lax.broadcasted_iota(jnp.int32, (16, chunk), 0) < 3).astype(F32).astype(BF16)

        def sine_of(t):
            e = 0.25 - jnp.abs(t - jnp.round(t))
            e2 = e * e
            acc = sine[-1]
            for term in sine[-2::-1]:
                acc = acc * e2 + term
            return (acc * e).astype(BF16)

        def filter_step(i, carry):
            start = pl.multiple_of(i * chunk, chunk)
            act_one = sine_of(dot(lift, feat[:, pl.ds(start, chunk)]))
            act_two = sine_of(dot(mix, jnp.concatenate([act_one, act_one, ones], axis=0)))
            raw = dot(pull, act_two)
            lag = (lax.broadcasted_iota(jnp.int32, (8, chunk), 1) + start).astype(F32)
            value = raw * jnp.exp(-rate * lag) * gain
            for q in range(chunk // LANES):
                row = pl.multiple_of((i * (chunk // LANES) + q) * 8, 8)
                filt[half, pl.ds(row, 8), :] = value[:, q * LANES : (q + 1) * LANES]
            return carry

        count = seq_len // chunk
        for part in range(2):
            lax.fori_loop(part * count // 2, (part + 1) * count // 2, filter_step, 0)
            if pass_on:
                pass_filter(part, 2)
        make_spectrum(half)

    early = my_z < n_ctx // 8

    pl.when(early)(functools.partial(make_filter, False))

    pl.semaphore_wait(barrier, n_ctx + n_ch - 2 + n_ch // 2)

    pltpu.make_async_copy(outgoing.at[mine], incoming.at[me], recv_sem).start()

    def send(x, z, core):
        pltpu.make_async_remote_copy(
            src_ref=outgoing.at[block_at(x, z, core)],
            dst_ref=incoming.at[me],
            send_sem=send_sem,
            recv_sem=recv_sem,
            device_id=(device_at(x, z, core), group),
            device_id_type=MESH,
        ).start()

    def send_far(e, carry):
        for off in (n_z // 2 - e, n_z // 2 + e):
            z = lax.rem(my_z + off, n_z)
            for_plane(z, send)
            send(my_x, z, half)
        return carry

    opposite = lax.rem(my_z + n_z // 2, n_z)
    for_plane(opposite, send)
    send(my_x, opposite, half)
    lax.fori_loop(1, n_z // 2, send_far, 0)
    for_plane(my_z, send)

    pltpu.make_async_remote_copy(
        src_ref=streams.at[2, pl.ds(tok - 8, 8)],
        dst_ref=halo,
        send_sem=halo_send,
        recv_sem=halo_recv,
        device_id=(ctx_peer(1), group),
        device_id_type=MESH,
    ).start()

    depth, cols_out = weight.shape[2], weight.shape[3]

    def weight_block(g):
        return weight_in.at[
            pl.ds(pl.multiple_of(half * depth, depth), depth),
            pl.ds(pl.multiple_of(g * cols_out, cols_out), cols_out),
        ]

    pltpu.make_async_copy(weight_block(group), weight.at[group, half], w_recv).start()
    for d in range(1, n_ch):
        pltpu.make_async_remote_copy(
            src_ref=weight_block(ch_peer(d)),
            dst_ref=weight.at[group, half],
            send_sem=w_send,
            recv_sem=w_recv,
            device_id=weight_peer(d),
            device_id_type=MESH,
        ).start()

    pl.when(early)(functools.partial(pass_filter, 0, 1))
    pl.when(jnp.logical_not(early))(functools.partial(make_filter, True))

    sent = filt.at[half]
    pltpu.make_async_copy(sent, sent, filt_send).wait()
    came = filt.at[1 - half]
    pltpu.make_async_copy(came, came, filt_recv).wait()
    make_spectrum(1 - half)

    def convolve(o, state):
        spec = forward((state.astype(BF16),))
        re, im = spec[:, :LANES], spec[:, LANES:]
        f_re, f_im = spectrum[o, :, :LANES], spectrum[o, :, LANES:]
        return inverse(jnp.concatenate([re * f_re - im * f_im, re * f_im + im * f_re], axis=1))

    row0 = lax.broadcasted_iota(jnp.int32, (n_ctx, LANES), 0) == 0
    lane_at = lax.broadcasted_iota(jnp.int32, (n_ctx, LANES), 1)

    def delayed(x, by):
        near = pltpu.roll(x, by, 1)
        carried = jnp.where(row0, 0.0, pltpu.roll(near, 1, 0))
        return jnp.where(lane_at < by, carried, near)

    def shortened(s):
        signal[s] = incoming[:, s].astype(F32).reshape(n_ctx * 4, tok)
        cols = []
        for c in range(4):
            x = signal[s, pl.ds(c, n_ctx, stride=4), :]
            taps = [picked(short[s, i : i + 1, :], c) for i in range(3)]
            cols.append(taps[0] * x + taps[1] * delayed(x, 1) + taps[2] * delayed(x, 2))
        return jnp.concatenate(cols, axis=1).astype(BF16).astype(F32)

    pltpu.make_async_copy(incoming, incoming, recv_sem).wait()
    state = shortened(0)
    for o in range(2):
        direct = jnp.concatenate(
            [jnp.broadcast_to(picked(skip[o : o + 1, :], c), (1, LANES)) for c in range(4)], axis=1
        )
        output = convolve(o, state) + direct * state
        if o == 0:
            state = (shortened(1) * output).astype(BF16).astype(F32)
    for c in range(4):
        signal[0, pl.ds(c, n_ctx, stride=4), :] = output[:, c * LANES : (c + 1) * LANES]
    back_out[...] = signal[0].reshape(n_ctx, 4, tok).astype(BF16)

    landing = back_in.at[my_class, lax.rem(mine, n_ctx // n_class)]
    pltpu.make_async_copy(back_out.at[me], landing, back_recv.at[my_class]).start()

    def send_back(x, z, core):
        place = device_at(x, z, core)
        pltpu.make_async_remote_copy(
            src_ref=back_out.at[place],
            dst_ref=landing,
            send_sem=back_send,
            recv_sem=back_recv.at[my_class],
            device_id=(place, group),
            device_id_type=MESH,
        ).start()

    def send_plane(z, carry):
        for_plane(z, send_back)

        @pl.when(z != my_z)
        def _():
            send_back(my_x, z, half)

        return carry

    lax.fori_loop(0, n_z, send_plane, 0)

    pltpu.make_async_copy(halo, halo, halo_recv).wait()
    near = streams[2].astype(F32)
    ahead = jnp.where(me > 0, halo[...].astype(F32), 0.0)
    at_row = lax.broadcasted_iota(jnp.int32, (tok, chl), 0)
    one = jnp.where(at_row == 0, ahead[7:8], pltpu.roll(near, 1, 0))
    two = jnp.where(at_row == 0, ahead[6:7], jnp.where(at_row == 1, ahead[7:8], pltpu.roll(near, 2, 0)))
    made = short[2, 0:1] * near + short[2, 1:2] * one + short[2, 2:3] * two
    gate[...] = dot_nt(turner, made.astype(BF16))

    for h in range(n_class):
        pltpu.make_async_copy(back_in.at[h], back_in.at[h], back_recv.at[h]).wait()
        block = back_in[h].astype(F32).reshape(class_rows, tok)
        rows = slice(h * class_rows, (h + 1) * class_rows)
        gathered[group, h] = (gate[rows, :] * block).astype(BF16)
        for hop in ring[::-1]:
            pltpu.make_async_remote_copy(
                src_ref=gathered.at[group, h],
                dst_ref=gathered.at[group, h],
                send_sem=ring_send.at[h],
                recv_sem=ring_recv.at[h, group],
                device_id=(me, ring_peer(hop)),
                device_id_type=MESH,
            ).start()
        if h == 0:
            pltpu.make_async_copy(weight.at[:, half], weight.at[:, half], w_recv).wait()
            swap = pltpu.make_async_remote_copy(
                src_ref=weight.at[:, half],
                dst_ref=weight.at[:, half],
                send_sem=pair_send,
                recv_sem=pair_recv,
                device_id=(partner, group),
                device_id_type=MESH,
            )
            swap.start()

    swap.wait()

    total = jnp.zeros((tok, cols_out), F32)
    per_half = n_class // 2
    for p in range(2):
        for hop in [(0, 0)] + ring:
            peer = ring_peer(hop)
            for h in range(p * per_half, (p + 1) * per_half):
                if hop != (0, 0):
                    came = gathered.at[peer, h]
                    pltpu.make_async_copy(came, came, ring_recv.at[h, peer]).wait()
            rows = gathered[peer, p * per_half : (p + 1) * per_half].reshape(wide_half, tok)
            total = total + dot(dot_nt(flip, rows).astype(BF16), weight[peer, p])
    out_ref[...] = total.astype(BF16)

    sent = outgoing.at[pl.ds(0, n_ctx - 1)]
    pltpu.make_async_copy(sent, sent, send_sem).wait()
    sent = back_out.at[pl.ds(0, n_ctx - 1)]
    pltpu.make_async_copy(sent, sent, back_send).wait()
    for h in range(n_class):
        sent = gathered.at[pl.ds(0, n_ch - 1), h]
        pltpu.make_async_copy(sent, sent, ring_send.at[h]).wait()
    pltpu.make_async_copy(halo, halo, halo_send).wait()
    sent = weight.at[pl.ds(0, n_ch - 1), half]
    pltpu.make_async_copy(sent, sent, w_send).wait()


def solution(mesh):
    n_ctx, n_ch = mesh.shape["ctx"], mesh.shape["ch"]

    def per_device(
        streams,
        short_weight,
        filt_first,
        filt_bias,
        filt_mid,
        filt_freq,
        filt_last,
        decay,
        skip,
        out_weight,
    ):
        tok, chl = streams.shape[1], streams.shape[2]
        seq_len = tok * n_ctx
        kept = (n_ctx + 1 + 7) // 8 * 8
        cols_out = out_weight.shape[1] // n_ch
        lead, tail, twiddle, wide = transform_tables(n_ctx, kept)
        feat = feature_table(seq_len)
        args = (
            streams,
            short_weight,
            jnp.transpose(filt_first, (1, 0, 2)),
            filt_bias,
            filt_mid,
            filt_freq,
            filt_last,
            decay,
            skip,
            out_weight,
            jnp.asarray(lead),
            jnp.asarray(tail),
            jnp.asarray(twiddle),
            jnp.asarray(wide),
            jnp.asarray(feat),
        )

        def vmem(x):
            return pltpu.VMEM(x.shape, x.dtype)

        staged = [vmem(args[i]) for i in (0, 1, 2, 3, 4, 5, 6, 7, 8, 10, 11, 12, 13, 14)]
        dma = pltpu.SemaphoreType.DMA
        return pl.pallas_call(
            functools.partial(kernel, n_ctx, n_ch, min(1024, seq_len // 2), sine_terms()),
            out_shape=pltpu.VMEM((tok, cols_out), BF16),
            in_specs=[pl.BlockSpec(memory_space=pl.ANY)] * len(args),
            out_specs=pl.BlockSpec(memory_space=pltpu.VMEM),
            scratch_shapes=staged
            + [
                pltpu.VMEM((n_ctx, 2, 4, tok), BF16),
                pltpu.VMEM((n_ctx, 2, 4, tok), BF16),
                pltpu.VMEM((2, n_ctx * 4, tok), F32),
                pltpu.VMEM((2, n_ctx * 8, LANES), F32),
                pltpu.VMEM((2, 4 * kept, 2 * LANES), F32),
                pltpu.VMEM((n_ctx, 4, tok), BF16),
                pltpu.VMEM((4, n_ctx // 4, 4, tok), BF16),
                pltpu.VMEM((n_ch, 4, chl // 4, tok), BF16),
                pltpu.VMEM((n_ch, 2, chl // 2, cols_out), BF16),
                pltpu.VMEM((8, chl), BF16),
                pltpu.VMEM((chl, tok), F32),
                dma((14,)),
                dma,
                dma,
                dma,
                dma((4,)),
                dma((4,)),
                dma((4, n_ch)),
                dma,
                dma,
                dma,
                dma,
                dma,
                dma,
                dma,
                dma,
            ],
            compiler_params=pltpu.CompilerParams(collective_id=0, has_side_effects=True),
        )(*args)

    return jax.shard_map(
        per_device,
        mesh=mesh,
        in_specs=(
            P(None, "ctx", "ch"),
            P(None, None, "ch"),
            P(),
            P(),
            P(),
            P(),
            P(None, None, "ch"),
            P(None, "ch"),
            P(None, "ch"),
            P("ch", None),
        ),
        out_specs=P("ctx", "ch"),
        check_vma=False,
    )
```

```python
import functools
import math

import jax
import jax.numpy as jnp
import numpy as np
from jax import lax
from jax.experimental import pallas as pl
from jax.experimental.pallas import tpu as pltpu
from jax.sharding import PartitionSpec as P

MESH = pl.DeviceIdType.MESH
BF16 = jnp.bfloat16
F32 = jnp.float32
EMB = 5
LANES = 128


def split_table(table):
    high = table.astype(np.float32).astype(jnp.bfloat16)
    low = (table - high.astype(np.float64)).astype(np.float32).astype(jnp.bfloat16)
    return np.stack([high, low])


def transform_tables(rows, kept):
    total = 2 * rows * LANES
    k = np.arange(kept)[:, None]
    live = k <= rows
    a = np.arange(rows)[None, :]
    b = np.arange(LANES)[None, :]
    angle = 2.0 * np.pi * ((k * a) % (2 * rows)) / (2 * rows)
    cos_a = np.where(live, np.cos(angle), 0.0)
    sin_a = np.where(live, np.sin(angle), 0.0)
    first = np.concatenate([cos_a, -sin_a], axis=0)
    weight = np.where((k == 0) | (k == rows), 1.0, 2.0) / total
    last = np.concatenate([(weight * cos_a).T, (-weight * sin_a).T], axis=1)
    turn = 2.0 * np.pi * ((k * b) % total) / total
    twiddle = np.stack([np.cos(turn), -np.sin(turn)]).astype(np.float32)
    j = np.arange(LANES)[:, None]
    phase = 2.0 * np.pi * ((j * b) % LANES) / LANES
    cos_b, sin_b = np.cos(phase), np.sin(phase)
    forward = np.block([[cos_b, -sin_b], [sin_b, cos_b]])
    wide = np.concatenate([split_table(forward), split_table(forward.T)])
    return split_table(first), split_table(last), twiddle, wide


def feature_table(seq_len):
    positions = np.arange(seq_len, dtype=np.int32)
    rows = [positions.astype(np.float32) / np.float32(seq_len)]
    cosines, sines = [], []
    for band in range((EMB - 1) // 2):
        wrapped = (band + 1) * positions % seq_len
        angle = np.float32(2.0 * math.pi / seq_len) * wrapped.astype(np.float32)
        cosines.append(np.cos(angle))
        sines.append(np.sin(angle))
    table = np.zeros((8, seq_len), np.float32)
    table[:EMB] = np.stack(rows + cosines + sines)
    table[EMB] = 1.0
    return np.concatenate([table] * 3).astype(jnp.bfloat16)


def sine_terms():
    e = 0.25 * np.cos(np.pi * (np.arange(400) + 0.5) / 800)
    basis = np.stack([e ** (2 * i + 1) for i in range(4)], axis=1)
    scale = 1.0 / np.maximum(np.abs(np.sin(2 * np.pi * e)), 1e-3)
    terms = np.linalg.lstsq(basis * scale[:, None], np.sin(2 * np.pi * e) * scale, rcond=None)[0]
    return [float(np.float32(t)) for t in terms]


def dot(a, b):
    return jnp.dot(a, b, preferred_element_type=F32)


def dot_nt(a, b):
    return lax.dot_general(a, b, (((1,), (1,)), ((), ())), preferred_element_type=F32)


def two_rows(a, b):
    both = dot(a, b)
    rows = a.shape[0] // 2
    return both[:rows] + both[rows:]


def halves(x):
    high = x.astype(BF16)
    return high, (x - high.astype(F32)).astype(BF16)


def eye(n, dtype):
    rows = lax.broadcasted_iota(jnp.int32, (n, n), 0)
    cols = lax.broadcasted_iota(jnp.int32, (n, n), 1)
    return (rows == cols).astype(F32).astype(dtype)


def terms(x, count):
    parts = []
    for _ in range(count):
        part = x.astype(BF16).astype(F32)
        parts.append(part)
        x = x - part
    return parts


def kernel(
    n_ctx,
    n_ch,
    chunk,
    sine,
    streams_in,
    short_in,
    first_in,
    bias_in,
    mid_in,
    freq_in,
    last_in,
    decay_in,
    skip_in,
    weight_in,
    lead_in,
    tail_in,
    twiddle_in,
    wide_in,
    feat_in,
    out_ref,
    streams,
    short,
    first,
    bias,
    mid,
    freq,
    last,
    decay,
    skip,
    lead,
    tail,
    twiddle,
    wide,
    feat,
    outgoing,
    incoming,
    signal,
    filt,
    spectrum,
    back_out,
    back_in,
    gathered,
    weight,
    halo,
    gate,
    load_sem,
    send_sem,
    recv_sem,
    back_send,
    back_recv,
    ring_send,
    ring_recv,
    w_send,
    w_recv,
    pair_send,
    pair_recv,
    filt_send,
    filt_recv,
    halo_send,
    halo_recv,
):
    me = lax.axis_index("ctx")
    group = lax.axis_index("ch")
    half = lax.rem(me, 2)
    partner = me + 1 - 2 * half
    tok, chl = streams.shape[1], streams.shape[2]
    wide_half = chl // 2
    kept = twiddle.shape[1]
    seq_len = feat.shape[1]

    def ctx_peer(d):
        return lax.rem(me + d, n_ctx)

    def ch_peer(d):
        return lax.rem(group + d, n_ch)

    n_y = n_ch // 2
    ring = [(dy, dx) for dy in range(n_y) for dx in range(2) if dy or dx]
    ring.sort(key=lambda p: min(p[0], n_y - p[0]) + 2 * p[1])

    def ring_peer(step):
        dy, dx = step
        return lax.rem(group // 2 + dy, n_y) * 2 + lax.rem(group + dx, 2)

    my_z = lax.rem(me, n_ctx // 2) // 2

    n_z = n_ctx // 4
    my_x = me // (2 * n_z)

    def device_at(x, z, core):
        return x * (2 * n_z) + 2 * z + core

    def block_at(x, z, core):
        far_side = z // (n_z // 2)
        fold = z + far_side * (n_z - 1 - 2 * z)
        return (2 * fold + far_side) * 4 + 2 * x + core

    mine = block_at(my_x, my_z, half)
    n_class = back_in.shape[0]
    class_rows = chl // n_class
    my_class = mine // (n_ctx // n_class)

    def for_plane(z, act):
        act(1 - my_x, z, 1 - half)
        act(1 - my_x, z, half)
        act(my_x, z, 1 - half)

    def weight_peer(d):
        return (ctx_peer(n_ctx // 2) if d % 2 else me, ch_peer(d))

    def for_ctx_peers(act):
        quarter = n_ctx // 4
        act(ctx_peer(quarter))
        act(ctx_peer(3 * quarter))

        def step(e, carry):
            act(ctx_peer(quarter + e))
            act(ctx_peer(quarter - e))
            act(ctx_peer(3 * quarter + e))
            act(ctx_peer(3 * quarter - e))
            return carry

        lax.fori_loop(1, quarter, step, 0)
        act(ctx_peer(2 * quarter))

    loads = []
    pairs = (
        (streams_in, streams),
        (feat_in, feat),
        (first_in, first),
        (bias_in, bias),
        (mid_in, mid),
        (freq_in, freq),
        (last_in, last),
        (decay_in, decay),
        (lead_in, lead),
        (twiddle_in, twiddle),
        (wide_in, wide),
        (short_in, short),
        (skip_in, skip),
        (tail_in, tail),
    )
    for i, (src, dst) in enumerate(pairs):
        copy = pltpu.make_async_copy(src, dst, load_sem.at[i])
        copy.start()
        loads.append(copy)

    barrier = pltpu.get_barrier_semaphore()

    def greet_ctx(peer):
        pl.semaphore_signal(barrier, inc=1, device_id=(peer, group), device_id_type=MESH)

    for_ctx_peers(greet_ctx)
    for d in range(1, n_ch):
        pl.semaphore_signal(barrier, inc=1, device_id=(me, ch_peer(d)), device_id_type=MESH)
        if d % 2:
            pl.semaphore_signal(barrier, inc=1, device_id=weight_peer(d), device_id_type=MESH)

    loads[0].wait()
    flip = eye(tok, BF16)
    turner = eye(chl, BF16)
    for s in range(2):
        turned = dot_nt(turner, streams[s])
        outgoing[:, s] = turned.reshape(n_ctx, 4, tok).astype(BF16)

    lane = lax.broadcasted_iota(jnp.int32, (1, chl), 1)

    def picked(row, c):
        return jnp.sum(jnp.where(lane == 4 * mine + c, row, 0.0), axis=1, keepdims=True)

    def forward(parts):
        high = parts[0]
        part = two_rows(lead[...].reshape(4 * kept, n_ctx), high)
        if len(parts) > 1:
            part = part + dot(lead[0], parts[1])
        rows = []
        for c in range(high.shape[1] // LANES):
            re = part[:kept, c * LANES : (c + 1) * LANES]
            im = part[kept:, c * LANES : (c + 1) * LANES]
            rows.append(jnp.concatenate([re * twiddle[0] - im * twiddle[1], re * twiddle[1] + im * twiddle[0]], axis=1))
        high, low = halves(jnp.concatenate(rows, axis=0))
        return two_rows(jnp.concatenate([high, low], axis=0), wide[0]) + dot(high, wide[1])

    def inverse(spec):
        high, low = halves(spec)
        part = two_rows(jnp.concatenate([high, low], axis=0), wide[2]) + dot(high, wide[3])
        cols = []
        for c in range(spec.shape[0] // kept):
            re = part[c * kept : (c + 1) * kept, :LANES]
            im = part[c * kept : (c + 1) * kept, LANES:]
            cols.append(jnp.concatenate([re * twiddle[0] + im * twiddle[1], im * twiddle[0] - re * twiddle[1]], axis=0))
        high, low = halves(jnp.concatenate(cols, axis=1))
        return two_rows(tail[...].reshape(2 * n_ctx, 2 * kept), high) + dot(tail[0], low)

    def make_spectrum(o):
        cols = [filt[o, pl.ds(4 * half + c, n_ctx, stride=8), :] for c in range(4)]
        spectrum[o] = forward(halves(jnp.concatenate(cols, axis=1)))

    def pass_filter(part, parts):
        rows = n_ctx * 8 // parts
        done = filt.at[half, pl.ds(part * rows, rows)]
        pltpu.make_async_remote_copy(
            src_ref=done,
            dst_ref=done,
            send_sem=filt_send,
            recv_sem=filt_recv,
            device_id=(partner, group),
            device_id_type=MESH,
        ).start()

    def make_filter(pass_on):
        for copy in loads[1:]:
            copy.wait()
        pick_rows = lax.broadcasted_iota(jnp.int32, (8, chl), 0)
        pick_cols = lax.broadcasted_iota(jnp.int32, (8, chl), 1)
        pick = jnp.zeros((8, chl), F32)
        for r in range(8):
            here = (pick_rows == r) & (pick_cols == 4 * (mine - half) + r)
            pick = jnp.where(here, 1.0, pick)

        hidden = mid.shape[1]
        turns = freq[pl.ds(half, 1), :] * (1.0 / (2.0 * math.pi))
        both = first[...].astype(F32)
        base = jnp.where(half == 0, both[:, 0, :], both[:, 1, :]) * turns
        shifts = bias[half] * turns - 0.25
        base = jnp.concatenate([base, shifts[0:1], jnp.zeros((8 - EMB - 1, hidden), F32)], axis=0)
        flip_h = eye(hidden, BF16)
        lift = dot_nt(flip_h, jnp.concatenate(terms(base, 3), axis=0).astype(BF16)).astype(BF16)
        mixed = terms(mid[half].astype(F32) * turns, 2)
        mixed = mixed + terms(shifts[1:2], 3) + [jnp.zeros((13, hidden), F32)]
        mix = dot_nt(flip_h, jnp.concatenate(mixed, axis=0).astype(BF16)).astype(BF16)
        pull = dot_nt(pick.astype(BF16), last[half]).astype(BF16)
        rate_row = jnp.where(pick > 0.0, decay[pl.ds(half, 1), :], 0.0)
        rate = jnp.sum(rate_row, axis=1, keepdims=True)
        gain = jnp.sqrt(2.0 * rate)
        ones = (lax.broadcasted_iota(jnp.int32, (16, chunk), 0) < 3).astype(F32).astype(BF16)

        def sine_of(t):
            e = 0.25 - jnp.abs(t - jnp.round(t))
            e2 = e * e
            acc = sine[-1]
            for term in sine[-2::-1]:
                acc = acc * e2 + term
            return (acc * e).astype(BF16)

        def filter_step(i, carry):
            start = pl.multiple_of(i * chunk, chunk)
            act_one = sine_of(dot(lift, feat[:, pl.ds(start, chunk)]))
            act_two = sine_of(dot(mix, jnp.concatenate([act_one, act_one, ones], axis=0)))
            raw = dot(pull, act_two)
            lag = (lax.broadcasted_iota(jnp.int32, (8, chunk), 1) + start).astype(F32)
            value = raw * jnp.exp(-rate * lag) * gain
            for q in range(chunk // LANES):
                row = pl.multiple_of((i * (chunk // LANES) + q) * 8, 8)
                filt[half, pl.ds(row, 8), :] = value[:, q * LANES : (q + 1) * LANES]
            return carry

        count = seq_len // chunk
        for part in range(2):
            lax.fori_loop(part * count // 2, (part + 1) * count // 2, filter_step, 0)
            if pass_on:
                pass_filter(part, 2)
        make_spectrum(half)

    early = my_z < n_ctx // 8

    pl.when(early)(functools.partial(make_filter, False))

    pl.semaphore_wait(barrier, n_ctx + n_ch - 2 + n_ch // 2)

    pltpu.make_async_copy(outgoing.at[mine], incoming.at[me], recv_sem).start()

    def send(x, z, core):
        pltpu.make_async_remote_copy(
            src_ref=outgoing.at[block_at(x, z, core)],
            dst_ref=incoming.at[me],
            send_sem=send_sem,
            recv_sem=recv_sem,
            device_id=(device_at(x, z, core), group),
            device_id_type=MESH,
        ).start()

    def send_far(e, carry):
        for off in (n_z // 2 - e, n_z // 2 + e):
            z = lax.rem(my_z + off, n_z)
            for_plane(z, send)
            send(my_x, z, half)
        return carry

    opposite = lax.rem(my_z + n_z // 2, n_z)
    for_plane(opposite, send)
    send(my_x, opposite, half)
    lax.fori_loop(1, n_z // 2, send_far, 0)
    for_plane(my_z, send)

    pltpu.make_async_remote_copy(
        src_ref=streams.at[2, pl.ds(tok - 8, 8)],
        dst_ref=halo,
        send_sem=halo_send,
        recv_sem=halo_recv,
        device_id=(ctx_peer(1), group),
        device_id_type=MESH,
    ).start()

    depth, cols_out = weight.shape[2], weight.shape[3]

    def weight_block(g):
        return weight_in.at[
            pl.ds(pl.multiple_of(half * depth, depth), depth),
            pl.ds(pl.multiple_of(g * cols_out, cols_out), cols_out),
        ]

    pltpu.make_async_copy(weight_block(group), weight.at[group, half], w_recv).start()
    for d in range(1, n_ch):
        pltpu.make_async_remote_copy(
            src_ref=weight_block(ch_peer(d)),
            dst_ref=weight.at[group, half],
            send_sem=w_send,
            recv_sem=w_recv,
            device_id=weight_peer(d),
            device_id_type=MESH,
        ).start()

    pl.when(early)(functools.partial(pass_filter, 0, 1))
    pl.when(jnp.logical_not(early))(functools.partial(make_filter, True))

    sent = filt.at[half]
    pltpu.make_async_copy(sent, sent, filt_send).wait()
    came = filt.at[1 - half]
    pltpu.make_async_copy(came, came, filt_recv).wait()
    make_spectrum(1 - half)

    def convolve(o, state):
        spec = forward((state.astype(BF16),))
        re, im = spec[:, :LANES], spec[:, LANES:]
        f_re, f_im = spectrum[o, :, :LANES], spectrum[o, :, LANES:]
        return inverse(jnp.concatenate([re * f_re - im * f_im, re * f_im + im * f_re], axis=1))

    row0 = lax.broadcasted_iota(jnp.int32, (n_ctx, LANES), 0) == 0
    lane_at = lax.broadcasted_iota(jnp.int32, (n_ctx, LANES), 1)

    def delayed(x, by):
        near = pltpu.roll(x, by, 1)
        carried = jnp.where(row0, 0.0, pltpu.roll(near, 1, 0))
        return jnp.where(lane_at < by, carried, near)

    def shortened(s):
        signal[s] = incoming[:, s].astype(F32).reshape(n_ctx * 4, tok)
        cols = []
        for c in range(4):
            x = signal[s, pl.ds(c, n_ctx, stride=4), :]
            taps = [picked(short[s, i : i + 1, :], c) for i in range(3)]
            cols.append(taps[0] * x + taps[1] * delayed(x, 1) + taps[2] * delayed(x, 2))
        return jnp.concatenate(cols, axis=1).astype(BF16).astype(F32)

    pltpu.make_async_copy(incoming, incoming, recv_sem).wait()
    state = shortened(0)
    for o in range(2):
        direct = jnp.concatenate(
            [jnp.broadcast_to(picked(skip[o : o + 1, :], c), (1, LANES)) for c in range(4)], axis=1
        )
        output = convolve(o, state) + direct * state
        if o == 0:
            state = (shortened(1) * output).astype(BF16).astype(F32)
    for c in range(4):
        signal[0, pl.ds(c, n_ctx, stride=4), :] = output[:, c * LANES : (c + 1) * LANES]
    back_out[...] = signal[0].reshape(n_ctx, 4, tok).astype(BF16)

    landing = back_in.at[my_class, lax.rem(mine, n_ctx // n_class)]
    pltpu.make_async_copy(back_out.at[me], landing, back_recv.at[my_class]).start()

    def send_back(x, z, core):
        place = device_at(x, z, core)
        pltpu.make_async_remote_copy(
            src_ref=back_out.at[place],
            dst_ref=landing,
            send_sem=back_send,
            recv_sem=back_recv.at[my_class],
            device_id=(place, group),
            device_id_type=MESH,
        ).start()

    def send_plane(z, carry):
        for_plane(z, send_back)

        @pl.when(z != my_z)
        def _():
            send_back(my_x, z, half)

        return carry

    lax.fori_loop(0, n_z, send_plane, 0)

    pltpu.make_async_copy(halo, halo, halo_recv).wait()
    near = streams[2].astype(F32)
    ahead = jnp.where(me > 0, halo[...].astype(F32), 0.0)
    at_row = lax.broadcasted_iota(jnp.int32, (tok, chl), 0)
    one = jnp.where(at_row == 0, ahead[7:8], pltpu.roll(near, 1, 0))
    two = jnp.where(at_row == 0, ahead[6:7], jnp.where(at_row == 1, ahead[7:8], pltpu.roll(near, 2, 0)))
    made = short[2, 0:1] * near + short[2, 1:2] * one + short[2, 2:3] * two
    gate[...] = dot_nt(turner, made.astype(BF16))

    for h in range(n_class):
        pltpu.make_async_copy(back_in.at[h], back_in.at[h], back_recv.at[h]).wait()
        block = back_in[h].astype(F32).reshape(class_rows, tok)
        rows = slice(h * class_rows, (h + 1) * class_rows)
        gathered[group, h] = (gate[rows, :] * block).astype(BF16)
        for hop in ring[::-1]:
            if h < 2 and hop[1] and hop[0]:
                continue
            pltpu.make_async_remote_copy(
                src_ref=gathered.at[group, h],
                dst_ref=gathered.at[group, h],
                send_sem=ring_send.at[h],
                recv_sem=ring_recv.at[h, group],
                device_id=(me, ring_peer(hop)),
                device_id_type=MESH,
            ).start()
        if h == 0:
            pltpu.make_async_copy(weight.at[:, half], weight.at[:, half], w_recv).wait()
            swap = pltpu.make_async_remote_copy(
                src_ref=weight.at[:, half],
                dst_ref=weight.at[:, half],
                send_sem=pair_send,
                recv_sem=pair_recv,
                device_id=(partner, group),
                device_id_type=MESH,
            )
            swap.start()

    beside = ring_peer((0, 1))
    for h in range(2):
        came = gathered.at[beside, h]
        pltpu.make_async_copy(came, came, ring_recv.at[h, beside]).wait()
        for hop in ring[::-1]:
            if hop[1] == 0:
                pltpu.make_async_remote_copy(
                    src_ref=gathered.at[beside, h],
                    dst_ref=gathered.at[beside, h],
                    send_sem=ring_send.at[h],
                    recv_sem=ring_recv.at[h, beside],
                    device_id=(me, ring_peer(hop)),
                    device_id_type=MESH,
                ).start()

    swap.wait()

    total = jnp.zeros((tok, cols_out), F32)
    for hop in [(0, 0)] + ring:
        peer = ring_peer(hop)
        if hop != (0, 0):
            for h in range(2 if hop == (0, 1) else 0, n_class):
                came = gathered.at[peer, h]
                pltpu.make_async_copy(came, came, ring_recv.at[h, peer]).wait()
        rows = dot_nt(flip, gathered[peer].reshape(chl, tok)).astype(BF16)
        total = total + dot(rows, weight[peer].reshape(chl, cols_out))
    out_ref[...] = total.astype(BF16)

    sent = outgoing.at[pl.ds(0, n_ctx - 1)]
    pltpu.make_async_copy(sent, sent, send_sem).wait()
    sent = back_out.at[pl.ds(0, n_ctx - 1)]
    pltpu.make_async_copy(sent, sent, back_send).wait()
    for h in range(n_class):
        sent = gathered.at[pl.ds(0, n_ch - 1), h]
        pltpu.make_async_copy(sent, sent, ring_send.at[h]).wait()
    pltpu.make_async_copy(halo, halo, halo_send).wait()
    sent = weight.at[pl.ds(0, n_ch - 1), half]
    pltpu.make_async_copy(sent, sent, w_send).wait()


def solution(mesh):
    n_ctx, n_ch = mesh.shape["ctx"], mesh.shape["ch"]

    def per_device(
        streams,
        short_weight,
        filt_first,
        filt_bias,
        filt_mid,
        filt_freq,
        filt_last,
        decay,
        skip,
        out_weight,
    ):
        tok, chl = streams.shape[1], streams.shape[2]
        seq_len = tok * n_ctx
        kept = (n_ctx + 1 + 7) // 8 * 8
        cols_out = out_weight.shape[1] // n_ch
        lead, tail, twiddle, wide = transform_tables(n_ctx, kept)
        feat = feature_table(seq_len)
        args = (
            streams,
            short_weight,
            jnp.transpose(filt_first, (1, 0, 2)),
            filt_bias,
            filt_mid,
            filt_freq,
            filt_last,
            decay,
            skip,
            out_weight,
            jnp.asarray(lead),
            jnp.asarray(tail),
            jnp.asarray(twiddle),
            jnp.asarray(wide),
            jnp.asarray(feat),
        )

        def vmem(x):
            return pltpu.VMEM(x.shape, x.dtype)

        staged = [vmem(args[i]) for i in (0, 1, 2, 3, 4, 5, 6, 7, 8, 10, 11, 12, 13, 14)]
        dma = pltpu.SemaphoreType.DMA
        return pl.pallas_call(
            functools.partial(kernel, n_ctx, n_ch, min(1024, seq_len // 2), sine_terms()),
            out_shape=pltpu.VMEM((tok, cols_out), BF16),
            in_specs=[pl.BlockSpec(memory_space=pl.ANY)] * len(args),
            out_specs=pl.BlockSpec(memory_space=pltpu.VMEM),
            scratch_shapes=staged
            + [
                pltpu.VMEM((n_ctx, 2, 4, tok), BF16),
                pltpu.VMEM((n_ctx, 2, 4, tok), BF16),
                pltpu.VMEM((2, n_ctx * 4, tok), F32),
                pltpu.VMEM((2, n_ctx * 8, LANES), F32),
                pltpu.VMEM((2, 4 * kept, 2 * LANES), F32),
                pltpu.VMEM((n_ctx, 4, tok), BF16),
                pltpu.VMEM((4, n_ctx // 4, 4, tok), BF16),
                pltpu.VMEM((n_ch, 4, chl // 4, tok), BF16),
                pltpu.VMEM((n_ch, 2, chl // 2, cols_out), BF16),
                pltpu.VMEM((8, chl), BF16),
                pltpu.VMEM((chl, tok), F32),
                dma((14,)),
                dma,
                dma,
                dma,
                dma((4,)),
                dma((4,)),
                dma((4, n_ch)),
                dma,
                dma,
                dma,
                dma,
                dma,
                dma,
                dma,
                dma,
            ],
            compiler_params=pltpu.CompilerParams(collective_id=0, has_side_effects=True),
        )(*args)

    return jax.shard_map(
        per_device,
        mesh=mesh,
        in_specs=(
            P(None, "ctx", "ch"),
            P(None, None, "ch"),
            P(),
            P(),
            P(),
            P(),
            P(None, None, "ch"),
            P(None, "ch"),
            P(None, "ch"),
            P("ch", None),
        ),
        out_specs=P("ctx", "ch"),
        check_vma=False,
    )
```

```python
import functools
import math

import jax
import jax.numpy as jnp
import numpy as np
from jax import lax
from jax.experimental import pallas as pl
from jax.experimental.pallas import tpu as pltpu
from jax.sharding import PartitionSpec as P

MESH = pl.DeviceIdType.MESH
BF16 = jnp.bfloat16
F32 = jnp.float32
EMB = 5
LANES = 128


def split_table(table):
    high = table.astype(np.float32).astype(jnp.bfloat16)
    low = (table - high.astype(np.float64)).astype(np.float32).astype(jnp.bfloat16)
    return np.stack([high, low])


def transform_tables(rows, kept):
    total = 2 * rows * LANES
    k = np.arange(kept)[:, None]
    live = k <= rows
    a = np.arange(rows)[None, :]
    b = np.arange(LANES)[None, :]
    angle = 2.0 * np.pi * ((k * a) % (2 * rows)) / (2 * rows)
    cos_a = np.where(live, np.cos(angle), 0.0)
    sin_a = np.where(live, np.sin(angle), 0.0)
    first = np.concatenate([cos_a, -sin_a], axis=0)
    weight = np.where((k == 0) | (k == rows), 1.0, 2.0) / total
    last = np.concatenate([(weight * cos_a).T, (-weight * sin_a).T], axis=1)
    turn = 2.0 * np.pi * ((k * b) % total) / total
    twiddle = np.stack([np.cos(turn), -np.sin(turn)]).astype(np.float32)
    j = np.arange(LANES)[:, None]
    phase = 2.0 * np.pi * ((j * b) % LANES) / LANES
    cos_b, sin_b = np.cos(phase), np.sin(phase)
    forward = np.block([[cos_b, -sin_b], [sin_b, cos_b]])
    wide = np.concatenate([split_table(forward), split_table(forward.T)])
    return split_table(first), split_table(last), twiddle, wide


def feature_table(seq_len):
    positions = np.arange(seq_len, dtype=np.int32)
    rows = [positions.astype(np.float32) / np.float32(seq_len)]
    cosines, sines = [], []
    for band in range((EMB - 1) // 2):
        wrapped = (band + 1) * positions % seq_len
        angle = np.float32(2.0 * math.pi / seq_len) * wrapped.astype(np.float32)
        cosines.append(np.cos(angle))
        sines.append(np.sin(angle))
    table = np.zeros((8, seq_len), np.float32)
    table[:EMB] = np.stack(rows + cosines + sines)
    table[EMB] = 1.0
    return np.concatenate([table] * 3).astype(jnp.bfloat16)


def sine_terms():
    e = 0.25 * np.cos(np.pi * (np.arange(400) + 0.5) / 800)
    basis = np.stack([e ** (2 * i + 1) for i in range(4)], axis=1)
    scale = 1.0 / np.maximum(np.abs(np.sin(2 * np.pi * e)), 1e-3)
    terms = np.linalg.lstsq(basis * scale[:, None], np.sin(2 * np.pi * e) * scale, rcond=None)[0]
    return [float(np.float32(t)) for t in terms]


def dot(a, b):
    return jnp.dot(a, b, preferred_element_type=F32)


def dot_nt(a, b):
    return lax.dot_general(a, b, (((1,), (1,)), ((), ())), preferred_element_type=F32)


def two_rows(a, b):
    both = dot(a, b)
    rows = a.shape[0] // 2
    return both[:rows] + both[rows:]


def halves(x):
    high = x.astype(BF16)
    return high, (x - high.astype(F32)).astype(BF16)


def eye(n, dtype):
    rows = lax.broadcasted_iota(jnp.int32, (n, n), 0)
    cols = lax.broadcasted_iota(jnp.int32, (n, n), 1)
    return (rows == cols).astype(F32).astype(dtype)


def terms(x, count):
    parts = []
    for _ in range(count):
        part = x.astype(BF16).astype(F32)
        parts.append(part)
        x = x - part
    return parts


def kernel(
    n_ctx,
    n_ch,
    chunk,
    sine,
    streams_in,
    short_in,
    first_in,
    bias_in,
    mid_in,
    freq_in,
    last_in,
    decay_in,
    skip_in,
    weight_in,
    lead_in,
    tail_in,
    twiddle_in,
    wide_in,
    feat_in,
    out_ref,
    streams,
    short,
    first,
    bias,
    mid,
    freq,
    last,
    decay,
    skip,
    lead,
    tail,
    twiddle,
    wide,
    feat,
    outgoing,
    incoming,
    signal,
    filt,
    spectrum,
    back_out,
    back_in,
    gathered,
    weight,
    halo,
    gate,
    load_sem,
    send_sem,
    recv_sem,
    back_send,
    back_recv,
    ring_send,
    ring_recv,
    w_send,
    w_recv,
    pair_send,
    pair_recv,
    filt_send,
    filt_recv,
    halo_send,
    halo_recv,
):
    me = lax.axis_index("ctx")
    group = lax.axis_index("ch")
    half = lax.rem(me, 2)
    partner = me + 1 - 2 * half
    tok, chl = streams.shape[1], streams.shape[2]
    wide_half = chl // 2
    kept = twiddle.shape[1]
    seq_len = feat.shape[1]

    def ctx_peer(d):
        return lax.rem(me + d, n_ctx)

    def ch_peer(d):
        return lax.rem(group + d, n_ch)

    n_y = n_ch // 2
    ring = [(dy, dx) for dy in range(n_y) for dx in range(2) if dy or dx]
    ring.sort(key=lambda p: min(p[0], n_y - p[0]) + 2 * p[1])

    def ring_peer(step):
        dy, dx = step
        return lax.rem(group // 2 + dy, n_y) * 2 + lax.rem(group + dx, 2)

    my_z = lax.rem(me, n_ctx // 2) // 2

    n_z = n_ctx // 4
    my_x = me // (2 * n_z)

    def device_at(x, z, core):
        return x * (2 * n_z) + 2 * z + core

    def block_at(x, z, core):
        far_side = z // (n_z // 2)
        fold = z + far_side * (n_z - 1 - 2 * z)
        return (2 * fold + far_side) * 4 + 2 * x + core

    mine = block_at(my_x, my_z, half)
    n_class = back_in.shape[0]
    class_rows = chl // n_class
    my_class = mine // (n_ctx // n_class)

    def for_plane(z, act):
        act(1 - my_x, z, 1 - half)
        act(1 - my_x, z, half)
        act(my_x, z, 1 - half)

    def weight_peer(d):
        return (ctx_peer(n_ctx // 2) if d % 2 else me, ch_peer(d))

    def for_ctx_peers(act):
        quarter = n_ctx // 4
        act(ctx_peer(quarter))
        act(ctx_peer(3 * quarter))

        def step(e, carry):
            act(ctx_peer(quarter + e))
            act(ctx_peer(quarter - e))
            act(ctx_peer(3 * quarter + e))
            act(ctx_peer(3 * quarter - e))
            return carry

        lax.fori_loop(1, quarter, step, 0)
        act(ctx_peer(2 * quarter))

    loads = []
    pairs = (
        (streams_in, streams),
        (feat_in, feat),
        (first_in, first),
        (bias_in, bias),
        (mid_in, mid),
        (freq_in, freq),
        (last_in, last),
        (decay_in, decay),
        (lead_in, lead),
        (twiddle_in, twiddle),
        (wide_in, wide),
        (short_in, short),
        (skip_in, skip),
        (tail_in, tail),
    )
    for i, (src, dst) in enumerate(pairs):
        copy = pltpu.make_async_copy(src, dst, load_sem.at[i])
        copy.start()
        loads.append(copy)

    barrier = pltpu.get_barrier_semaphore()

    def greet_ctx(peer):
        pl.semaphore_signal(barrier, inc=1, device_id=(peer, group), device_id_type=MESH)

    for_ctx_peers(greet_ctx)
    for d in range(1, n_ch):
        pl.semaphore_signal(barrier, inc=1, device_id=(me, ch_peer(d)), device_id_type=MESH)
        if d % 2:
            pl.semaphore_signal(barrier, inc=1, device_id=weight_peer(d), device_id_type=MESH)

    loads[0].wait()
    flip = eye(tok, BF16)
    turner = eye(chl, BF16)
    for s in range(2):
        turned = dot_nt(turner, streams[s])
        outgoing[:, s] = turned.reshape(n_ctx, 4, tok).astype(BF16)

    lane = lax.broadcasted_iota(jnp.int32, (1, chl), 1)

    def picked(row, c):
        return jnp.sum(jnp.where(lane == 4 * mine + c, row, 0.0), axis=1, keepdims=True)

    def forward(parts):
        high = parts[0]
        part = two_rows(lead[...].reshape(4 * kept, n_ctx), high)
        if len(parts) > 1:
            part = part + dot(lead[0], parts[1])
        rows = []
        for c in range(high.shape[1] // LANES):
            re = part[:kept, c * LANES : (c + 1) * LANES]
            im = part[kept:, c * LANES : (c + 1) * LANES]
            rows.append(jnp.concatenate([re * twiddle[0] - im * twiddle[1], re * twiddle[1] + im * twiddle[0]], axis=1))
        high, low = halves(jnp.concatenate(rows, axis=0))
        return two_rows(jnp.concatenate([high, low], axis=0), wide[0]) + dot(high, wide[1])

    def inverse(spec):
        high, low = halves(spec)
        part = two_rows(jnp.concatenate([high, low], axis=0), wide[2]) + dot(high, wide[3])
        cols = []
        for c in range(spec.shape[0] // kept):
            re = part[c * kept : (c + 1) * kept, :LANES]
            im = part[c * kept : (c + 1) * kept, LANES:]
            cols.append(jnp.concatenate([re * twiddle[0] + im * twiddle[1], im * twiddle[0] - re * twiddle[1]], axis=0))
        high, low = halves(jnp.concatenate(cols, axis=1))
        return two_rows(tail[...].reshape(2 * n_ctx, 2 * kept), high) + dot(tail[0], low)

    def make_spectrum(o):
        cols = [filt[o, pl.ds(4 * half + c, n_ctx, stride=8), :] for c in range(4)]
        spectrum[o] = forward(halves(jnp.concatenate(cols, axis=1)))

    def pass_filter(part, parts):
        rows = n_ctx * 8 // parts
        done = filt.at[half, pl.ds(part * rows, rows)]
        pltpu.make_async_remote_copy(
            src_ref=done,
            dst_ref=done,
            send_sem=filt_send,
            recv_sem=filt_recv,
            device_id=(partner, group),
            device_id_type=MESH,
        ).start()

    def make_filter(pass_on):
        for copy in loads[1:]:
            copy.wait()
        pick_rows = lax.broadcasted_iota(jnp.int32, (8, chl), 0)
        pick_cols = lax.broadcasted_iota(jnp.int32, (8, chl), 1)
        pick = jnp.zeros((8, chl), F32)
        for r in range(8):
            here = (pick_rows == r) & (pick_cols == 4 * (mine - half) + r)
            pick = jnp.where(here, 1.0, pick)

        hidden = mid.shape[1]
        turns = freq[pl.ds(half, 1), :] * (1.0 / (2.0 * math.pi))
        both = first[...].astype(F32)
        base = jnp.where(half == 0, both[:, 0, :], both[:, 1, :]) * turns
        shifts = bias[half] * turns - 0.25
        base = jnp.concatenate([base, shifts[0:1], jnp.zeros((8 - EMB - 1, hidden), F32)], axis=0)
        flip_h = eye(hidden, BF16)
        lift = dot_nt(flip_h, jnp.concatenate(terms(base, 3), axis=0).astype(BF16)).astype(BF16)
        mixed = terms(mid[half].astype(F32) * turns, 2)
        mixed = mixed + terms(shifts[1:2], 3) + [jnp.zeros((13, hidden), F32)]
        mix = dot_nt(flip_h, jnp.concatenate(mixed, axis=0).astype(BF16)).astype(BF16)
        pull = dot_nt(pick.astype(BF16), last[half]).astype(BF16)
        rate_row = jnp.where(pick > 0.0, decay[pl.ds(half, 1), :], 0.0)
        rate = jnp.sum(rate_row, axis=1, keepdims=True)
        gain = jnp.sqrt(2.0 * rate)
        ones = (lax.broadcasted_iota(jnp.int32, (16, chunk), 0) < 3).astype(F32).astype(BF16)

        def sine_of(t):
            e = 0.25 - jnp.abs(t - jnp.round(t))
            e2 = e * e
            acc = sine[-1]
            for term in sine[-2::-1]:
                acc = acc * e2 + term
            return (acc * e).astype(BF16)

        def filter_step(i, carry):
            start = pl.multiple_of(i * chunk, chunk)
            act_one = sine_of(dot(lift, feat[:, pl.ds(start, chunk)]))
            act_two = sine_of(dot(mix, jnp.concatenate([act_one, act_one, ones], axis=0)))
            raw = dot(pull, act_two)
            lag = (lax.broadcasted_iota(jnp.int32, (8, chunk), 1) + start).astype(F32)
            value = raw * jnp.exp(-rate * lag) * gain
            for q in range(chunk // LANES):
                row = pl.multiple_of((i * (chunk // LANES) + q) * 8, 8)
                filt[half, pl.ds(row, 8), :] = value[:, q * LANES : (q + 1) * LANES]
            return carry

        count = seq_len // chunk
        for part in range(2):
            lax.fori_loop(part * count // 2, (part + 1) * count // 2, filter_step, 0)
            if pass_on:
                pass_filter(part, 2)
        make_spectrum(half)

    early = my_z < n_ctx // 8

    pl.when(early)(functools.partial(make_filter, False))

    pl.semaphore_wait(barrier, n_ctx + n_ch - 2 + n_ch // 2)

    pltpu.make_async_copy(outgoing.at[mine], incoming.at[me], recv_sem).start()

    def send(x, z, core):
        pltpu.make_async_remote_copy(
            src_ref=outgoing.at[block_at(x, z, core)],
            dst_ref=incoming.at[me],
            send_sem=send_sem,
            recv_sem=recv_sem,
            device_id=(device_at(x, z, core), group),
            device_id_type=MESH,
        ).start()

    def send_far(e, carry):
        for off in (n_z // 2 - e, n_z // 2 + e):
            z = lax.rem(my_z + off, n_z)
            for_plane(z, send)
            send(my_x, z, half)
        return carry

    opposite = lax.rem(my_z + n_z // 2, n_z)
    for_plane(opposite, send)
    send(my_x, opposite, half)
    lax.fori_loop(1, n_z // 2, send_far, 0)
    for_plane(my_z, send)

    pltpu.make_async_remote_copy(
        src_ref=streams.at[2, pl.ds(tok - 8, 8)],
        dst_ref=halo,
        send_sem=halo_send,
        recv_sem=halo_recv,
        device_id=(ctx_peer(1), group),
        device_id_type=MESH,
    ).start()

    depth, cols_out = weight.shape[2], weight.shape[3]

    pl.when(early)(functools.partial(pass_filter, 0, 1))
    pl.when(jnp.logical_not(early))(functools.partial(make_filter, True))

    sent = filt.at[half]
    pltpu.make_async_copy(sent, sent, filt_send).wait()
    came = filt.at[1 - half]
    pltpu.make_async_copy(came, came, filt_recv).wait()
    make_spectrum(1 - half)

    def convolve(o, state):
        spec = forward((state.astype(BF16),))
        re, im = spec[:, :LANES], spec[:, LANES:]
        f_re, f_im = spectrum[o, :, :LANES], spectrum[o, :, LANES:]
        return inverse(jnp.concatenate([re * f_re - im * f_im, re * f_im + im * f_re], axis=1))

    def weight_block(g):
        return weight_in.at[
            pl.ds(pl.multiple_of(half * depth, depth), depth),
            pl.ds(pl.multiple_of(g * cols_out, cols_out), cols_out),
        ]

    pltpu.make_async_copy(weight_block(group), weight.at[group, half], w_recv).start()
    for d in range(1, n_ch):
        pltpu.make_async_remote_copy(
            src_ref=weight_block(ch_peer(d)),
            dst_ref=weight.at[group, half],
            send_sem=w_send,
            recv_sem=w_recv,
            device_id=weight_peer(d),
            device_id_type=MESH,
        ).start()

    row0 = lax.broadcasted_iota(jnp.int32, (n_ctx, LANES), 0) == 0
    lane_at = lax.broadcasted_iota(jnp.int32, (n_ctx, LANES), 1)

    def delayed(x, by):
        near = pltpu.roll(x, by, 1)
        carried = jnp.where(row0, 0.0, pltpu.roll(near, 1, 0))
        return jnp.where(lane_at < by, carried, near)

    def shortened(s):
        signal[s] = incoming[:, s].astype(F32).reshape(n_ctx * 4, tok)
        cols = []
        for c in range(4):
            x = signal[s, pl.ds(c, n_ctx, stride=4), :]
            taps = [picked(short[s, i : i + 1, :], c) for i in range(3)]
            cols.append(taps[0] * x + taps[1] * delayed(x, 1) + taps[2] * delayed(x, 2))
        return jnp.concatenate(cols, axis=1).astype(BF16).astype(F32)

    pltpu.make_async_copy(incoming, incoming, recv_sem).wait()
    state = shortened(0)
    for o in range(2):
        direct = jnp.concatenate(
            [jnp.broadcast_to(picked(skip[o : o + 1, :], c), (1, LANES)) for c in range(4)], axis=1
        )
        output = convolve(o, state) + direct * state
        if o == 0:
            state = (shortened(1) * output).astype(BF16).astype(F32)
    for c in range(4):
        signal[0, pl.ds(c, n_ctx, stride=4), :] = output[:, c * LANES : (c + 1) * LANES]
    back_out[...] = signal[0].reshape(n_ctx, 4, tok).astype(BF16)

    landing = back_in.at[my_class, lax.rem(mine, n_ctx // n_class)]
    pltpu.make_async_copy(back_out.at[me], landing, back_recv.at[my_class]).start()

    def send_back(x, z, core):
        place = device_at(x, z, core)
        pltpu.make_async_remote_copy(
            src_ref=back_out.at[place],
            dst_ref=landing,
            send_sem=back_send,
            recv_sem=back_recv.at[my_class],
            device_id=(place, group),
            device_id_type=MESH,
        ).start()

    def send_plane(z, carry):
        for_plane(z, send_back)

        @pl.when(z != my_z)
        def _():
            send_back(my_x, z, half)

        return carry

    lax.fori_loop(0, n_z, send_plane, 0)

    pltpu.make_async_copy(halo, halo, halo_recv).wait()
    near = streams[2].astype(F32)
    ahead = jnp.where(me > 0, halo[...].astype(F32), 0.0)
    at_row = lax.broadcasted_iota(jnp.int32, (tok, chl), 0)
    one = jnp.where(at_row == 0, ahead[7:8], pltpu.roll(near, 1, 0))
    two = jnp.where(at_row == 0, ahead[6:7], jnp.where(at_row == 1, ahead[7:8], pltpu.roll(near, 2, 0)))
    made = short[2, 0:1] * near + short[2, 1:2] * one + short[2, 2:3] * two
    gate[...] = dot_nt(turner, made.astype(BF16))

    for h in range(n_class):
        pltpu.make_async_copy(back_in.at[h], back_in.at[h], back_recv.at[h]).wait()
        block = back_in[h].astype(F32).reshape(class_rows, tok)
        rows = slice(h * class_rows, (h + 1) * class_rows)
        gathered[group, h] = (gate[rows, :] * block).astype(BF16)
        for hop in ring[::-1]:
            pltpu.make_async_remote_copy(
                src_ref=gathered.at[group, h],
                dst_ref=gathered.at[group, h],
                send_sem=ring_send.at[h],
                recv_sem=ring_recv.at[h, group],
                device_id=(me, ring_peer(hop)),
                device_id_type=MESH,
            ).start()

    pltpu.make_async_copy(weight.at[:, half], weight.at[:, half], w_recv).wait()
    swap = pltpu.make_async_remote_copy(
        src_ref=weight.at[:, half],
        dst_ref=weight.at[:, half],
        send_sem=pair_send,
        recv_sem=pair_recv,
        device_id=(partner, group),
        device_id_type=MESH,
    )
    swap.start()

    swap.wait()

    total = jnp.zeros((tok, cols_out), F32)
    for hop in [(0, 0)] + ring:
        peer = ring_peer(hop)
        if hop != (0, 0):
            for h in range(n_class):
                came = gathered.at[peer, h]
                pltpu.make_async_copy(came, came, ring_recv.at[h, peer]).wait()
        rows = dot_nt(flip, gathered[peer].reshape(chl, tok)).astype(BF16)
        total = total + dot(rows, weight[peer].reshape(chl, cols_out))
    out_ref[...] = total.astype(BF16)

    sent = outgoing.at[pl.ds(0, n_ctx - 1)]
    pltpu.make_async_copy(sent, sent, send_sem).wait()
    sent = back_out.at[pl.ds(0, n_ctx - 1)]
    pltpu.make_async_copy(sent, sent, back_send).wait()
    for h in range(n_class):
        sent = gathered.at[pl.ds(0, n_ch - 1), h]
        pltpu.make_async_copy(sent, sent, ring_send.at[h]).wait()
    pltpu.make_async_copy(halo, halo, halo_send).wait()
    sent = weight.at[pl.ds(0, n_ch - 1), half]
    pltpu.make_async_copy(sent, sent, w_send).wait()


def solution(mesh):
    n_ctx, n_ch = mesh.shape["ctx"], mesh.shape["ch"]

    def per_device(
        streams,
        short_weight,
        filt_first,
        filt_bias,
        filt_mid,
        filt_freq,
        filt_last,
        decay,
        skip,
        out_weight,
    ):
        tok, chl = streams.shape[1], streams.shape[2]
        seq_len = tok * n_ctx
        kept = (n_ctx + 1 + 7) // 8 * 8
        cols_out = out_weight.shape[1] // n_ch
        lead, tail, twiddle, wide = transform_tables(n_ctx, kept)
        feat = feature_table(seq_len)
        args = (
            streams,
            short_weight,
            jnp.transpose(filt_first, (1, 0, 2)),
            filt_bias,
            filt_mid,
            filt_freq,
            filt_last,
            decay,
            skip,
            out_weight,
            jnp.asarray(lead),
            jnp.asarray(tail),
            jnp.asarray(twiddle),
            jnp.asarray(wide),
            jnp.asarray(feat),
        )

        def vmem(x):
            return pltpu.VMEM(x.shape, x.dtype)

        staged = [vmem(args[i]) for i in (0, 1, 2, 3, 4, 5, 6, 7, 8, 10, 11, 12, 13, 14)]
        dma = pltpu.SemaphoreType.DMA
        return pl.pallas_call(
            functools.partial(kernel, n_ctx, n_ch, min(1024, seq_len // 2), sine_terms()),
            out_shape=pltpu.VMEM((tok, cols_out), BF16),
            in_specs=[pl.BlockSpec(memory_space=pl.ANY)] * len(args),
            out_specs=pl.BlockSpec(memory_space=pltpu.VMEM),
            scratch_shapes=staged
            + [
                pltpu.VMEM((n_ctx, 2, 4, tok), BF16),
                pltpu.VMEM((n_ctx, 2, 4, tok), BF16),
                pltpu.VMEM((2, n_ctx * 4, tok), F32),
                pltpu.VMEM((2, n_ctx * 8, LANES), F32),
                pltpu.VMEM((2, 4 * kept, 2 * LANES), F32),
                pltpu.VMEM((n_ctx, 4, tok), BF16),
                pltpu.VMEM((4, n_ctx // 4, 4, tok), BF16),
                pltpu.VMEM((n_ch, 4, chl // 4, tok), BF16),
                pltpu.VMEM((n_ch, 2, chl // 2, cols_out), BF16),
                pltpu.VMEM((8, chl), BF16),
                pltpu.VMEM((chl, tok), F32),
                dma((14,)),
                dma,
                dma,
                dma,
                dma((4,)),
                dma((4,)),
                dma((4, n_ch)),
                dma,
                dma,
                dma,
                dma,
                dma,
                dma,
                dma,
                dma,
            ],
            compiler_params=pltpu.CompilerParams(collective_id=0, has_side_effects=True),
        )(*args)

    return jax.shard_map(
        per_device,
        mesh=mesh,
        in_specs=(
            P(None, "ctx", "ch"),
            P(None, None, "ch"),
            P(),
            P(),
            P(),
            P(),
            P(None, None, "ch"),
            P(None, "ch"),
            P(None, "ch"),
            P("ch", None),
        ),
        out_specs=P("ctx", "ch"),
        check_vma=False,
    )
```
